32 devices in a mesh: gx: 4 (over y, x), gy: 8 (over z, core).
Axes of the slice: x: 2, y: 2, z: 4, core: 2. Of those that a mesh axis runs over, the one named last changes fastest.
Arguments:
- thermal_field: bfloat16 [384, 384, 128], P('gx', 'gy'), may hold values from -6 to 6
- probe_range_east: bfloat16 [384, 128], P('gx'), may hold values from -0.3125 to 0.3125
- probe_range_north: bfloat16 [384, 128], P('gy'), may hold values from -0.3125 to 0.3125
- probe_range_upward: bfloat16 [128, 128], replicated, may hold values from -0.5 to 0.5
- gauss_kernel_east: bfloat16 [384, 384], replicated, may hold values from -0.3125 to 0.3125
- gauss_kernel_north: bfloat16 [384, 384], replicated, may hold values from -0.3125 to 0.3125
- gauss_kernel_upward: bfloat16 [384, 128], replicated, may hold values from -0.5 to 0.5
Outputs:
- factor_x: float32 [384, 128], P('gx')
- factor_y: float32 [384, 128], P('gy')
- factor_z: float32 [128, 128], replicated
- core_sketch: float32 [384, 384, 384], P('gx', None, 'gy')
The draws below stay inside these ranges and needn't reach their ends.
All inputs are finite; a program needn't handle non-finite values.
Results may differ from the reference program's by a relative error of at most 0.0029.
Values may be sent and summed in bfloat16 or wider, within the bound.
A program may use at most 64 MiB of HBM per device.

```python
import jax
import jax.numpy as jnp
from jax import lax

POINTS_IN_SHARD = 96
SHEET_HEIGHT_UP = 128
K = 128
S = 384
MESH_WIDTH_EAST = 384
MESH_WIDTH_NORTH = 384
N_GX = 4


def steps_of(stream_key, dims, shards, smallest, largest):
    gain = 1.0
    for position, shards_of in shards:
        draws = jax.random.uniform(jax.random.fold_in(jax.random.fold_in(stream_key, 6), position), (shards_of,), jnp.float32, smallest / len(shards), largest / len(shards))
        gain = gain * jnp.repeat(jnp.exp(draws), dims[position] // shards_of).reshape((-1,) + (1,) * (len(dims) - 1 - position))
    return gain


def gaussian(stream_key, shape, scale, reach, split=(), kind=jnp.bfloat16):
    values = scale * jax.random.normal(stream_key, shape, jnp.float32)
    if split:
        values = values * steps_of(stream_key, shape, split, -0.22, 0.18)
    return jnp.clip(values, -reach, reach).astype(kind)


def setup_inputs(seed: int = 0) -> dict:
    streams_of = jax.random.split(jax.random.key(seed), 8)
    return {
        "thermal_field": gaussian(streams_of[0], (MESH_WIDTH_EAST, MESH_WIDTH_NORTH, SHEET_HEIGHT_UP), 1.0, 6.0, ((0, 4), (1, 8))),
        "probe_range_east": gaussian(streams_of[1], (MESH_WIDTH_EAST, K), MESH_WIDTH_EAST ** -0.5, 0.3125, ((0, 4),)),
        "probe_range_north": gaussian(streams_of[2], (MESH_WIDTH_NORTH, K), MESH_WIDTH_NORTH ** -0.5, 0.3125, ((0, 8),)),
        "probe_range_upward": gaussian(streams_of[3], (SHEET_HEIGHT_UP, K), SHEET_HEIGHT_UP ** -0.5, 0.5),
        "gauss_kernel_east": gaussian(streams_of[4], (S, MESH_WIDTH_EAST), MESH_WIDTH_EAST ** -0.5, 0.3125),
        "gauss_kernel_north": gaussian(streams_of[5], (S, MESH_WIDTH_NORTH), MESH_WIDTH_NORTH ** -0.5, 0.3125),
        "gauss_kernel_upward": gaussian(streams_of[6], (S, SHEET_HEIGHT_UP), SHEET_HEIGHT_UP ** -0.5, 0.5),
    }


def reference(thermal_field, probe_range_east, probe_range_north, probe_range_upward, gauss_kernel_east, gauss_kernel_north, gauss_kernel_upward):
    highest = lax.Precision.HIGHEST
    width = probe_range_upward.shape[1]
    along_x = probe_range_east.astype(jnp.float32)
    along_y = probe_range_north.astype(jnp.float32)

    def block(carry, index):
        part_y, part_z = carry
        opening_offset = (index * POINTS_IN_SHARD).astype(jnp.int32)
        point_total = lax.dynamic_slice_in_dim(thermal_field, opening_offset, POINTS_IN_SHARD, 0)
        rows_x = lax.dynamic_slice_in_dim(along_x, opening_offset, POINTS_IN_SHARD, 0)
        unrolled_tensor = point_total.reshape(POINTS_IN_SHARD * MESH_WIDTH_NORTH, SHEET_HEIGHT_UP)
        weighted = jnp.dot(unrolled_tensor, probe_range_upward, preferred_element_type=jnp.float32).reshape(POINTS_IN_SHARD, MESH_WIDTH_NORTH, width)
        factor_rows = jnp.sum(weighted * along_y[None, :, :], axis=1)
        part_y = part_y + jnp.sum(weighted * rows_x[:, None, :], axis=0)
        khatri = (rows_x[:, None, :] * along_y[None, :, :]).astype(jnp.bfloat16).reshape(POINTS_IN_SHARD * MESH_WIDTH_NORTH, width)
        part_z = part_z + jnp.dot(unrolled_tensor.T, khatri, preferred_element_type=jnp.float32)
        return (part_y, part_z), factor_rows

    start_carry = (jnp.zeros((MESH_WIDTH_NORTH, width), jnp.float32), jnp.zeros((SHEET_HEIGHT_UP, width), jnp.float32))
    (factor_y, factor_z), blocks = lax.scan(block, start_carry, jnp.arange(N_GX, dtype=jnp.int32))
    factor_x = blocks.reshape(MESH_WIDTH_EAST, width)

    leading_offset = jnp.dot(gauss_kernel_east, thermal_field.reshape(MESH_WIDTH_EAST, MESH_WIDTH_NORTH * SHEET_HEIGHT_UP), preferred_element_type=jnp.float32)
    leading_offset = leading_offset.reshape(S, MESH_WIDTH_NORTH, SHEET_HEIGHT_UP)
    second = jnp.einsum("ajl,bj->abl", leading_offset, gauss_kernel_north.astype(jnp.float32), precision=highest)
    core_sketch = jnp.einsum("abl,cl->abc", second, gauss_kernel_upward.astype(jnp.float32), precision=highest)
    return factor_x, factor_y, factor_z, core_sketch
```

```python
import functools

import jax
import jax.numpy as jnp
import numpy as np
from jax import lax
from jax.experimental import pallas as pl
from jax.experimental.pallas import tpu as pltpu
from jax.sharding import PartitionSpec as P

MESH = pl.DeviceIdType.MESH
VMEM = pl.BlockSpec(memory_space=pltpu.VMEM)
ANY = pl.BlockSpec(memory_space=pl.ANY)
BF = jnp.bfloat16
F32 = jnp.float32


def remote(src, dst, send, recv, where):
    copy = pltpu.make_async_remote_copy(
        src_ref=src, dst_ref=dst, send_sem=send, recv_sem=recv, device_id=where, device_id_type=MESH
    )
    copy.start()
    return copy


def sketch_parts(f_ref, east_ref, north_ref, up_ref, q_ref, py_ref, px_buf):
    rows, span, deep = f_ref.shape
    width = up_ref.shape[1]
    step = 16 if rows % 16 == 0 else rows
    along_y = north_ref[...].astype(F32)
    part_y = jnp.zeros((span, width), F32)
    part_z = jnp.zeros((deep, width), F32)
    for c in range(0, rows, step):
        cells = f_ref[c : c + step].reshape(step * span, deep)
        along_x = east_ref[c : c + step].astype(F32)
        weighted = jnp.dot(cells, up_ref[...], preferred_element_type=F32).reshape(step, span, width)
        px_buf[c : c + step] = jnp.sum(weighted * along_y[None, :, :], axis=1)
        part_y = part_y + jnp.sum(weighted * along_x[:, None, :], axis=0)
        khatri = (along_x[:, None, :] * along_y[None, :, :]).astype(BF).reshape(step * span, width)
        part_z = part_z + lax.dot_general(
            cells, khatri, (((0,), (0,)), ((), ())), preferred_element_type=F32
        )
    py_ref[...] = part_y
    ny = q_ref.shape[0]
    x_rows, z_rows = rows // ny, deep // ny
    for k in range(ny):
        q_ref[k, :x_rows] = px_buf[k * x_rows : (k + 1) * x_rows]
        q_ref[k, x_rows:] = part_z[k * z_rows : (k + 1) * z_rows]


def mix_x_kernel(
    n, chunks, t_ref, g_ref, f_ref, east_ref, north_ref, up_ref, w_ref, q_ref, py_ref,
    x_buf, y_buf, px_buf, s1, r1, s2, r2, ls,
):
    gx, gy = lax.axis_index("gx"), lax.axis_index("gy")
    rows = t_ref.shape[0]
    a_rows = y_buf.shape[2]
    wide = t_ref.shape[1] // n
    part = wide // chunks
    barrier = pltpu.get_barrier_semaphore()
    for d in range(1, n):
        pl.semaphore_signal(barrier, inc=1, device_id=(lax.rem(gx + d, n), gy), device_id_type=MESH)
    pl.semaphore_wait(barrier, n - 1)

    first, second, local = [], [], []
    for m in range(chunks):
        for d in range(1, n):
            to = lax.rem(gx + d, n)
            lanes = pl.ds(pl.multiple_of(to * wide + m * part, 128), part)
            first.append(
                remote(t_ref.at[:, lanes], x_buf.at[m, gx], s1.at[m, d], r1.at[m, d], (to, gy))
            )
        lanes = pl.ds(pl.multiple_of(gx * wide + m * part, 128), part)
        own = pltpu.make_async_copy(t_ref.at[:, lanes], x_buf.at[m, gx], ls.at[m, 0])
        own.start()
        local.append(own)
    sketch_parts(f_ref, east_ref, north_ref, up_ref, q_ref, py_ref, px_buf)
    for m in range(chunks):
        local[m].wait()
        for d in range(1, n):
            first[m * (n - 1) + d - 1].wait()
        block = x_buf[m].reshape(n * rows, part)
        lanes = pl.ds(pl.multiple_of(gx * wide + m * part, 128), part)
        for d in range(1, n + 1):
            to = lax.rem(gx + d, n)
            y_buf[m, d - 1] = jnp.dot(g_ref[to], block, preferred_element_type=F32).astype(BF)
            if d < n:
                second.append(
                    remote(
                        y_buf.at[m, d - 1], w_ref.at[:, lanes], s2.at[m, d], r2.at[m, d], (to, gy)
                    )
                )
            else:
                own = pltpu.make_async_copy(y_buf.at[m, d - 1], w_ref.at[:, lanes], ls.at[m, 1])
                own.start()
                second.append(own)
    for copy in second:
        copy.wait()


def mix_x(field, gauss, n, a_rows, cells, east, north, up, ny):
    rows, lanes = field.shape
    wide = lanes // n
    chunks = 3 if wide % 384 == 0 else 1
    dma = lambda *shape: pltpu.SemaphoreType.DMA(shape)
    return pl.pallas_call(
        functools.partial(mix_x_kernel, n, chunks),
        out_shape=(
            jax.ShapeDtypeStruct((a_rows, lanes), BF),
            jax.ShapeDtypeStruct((ny, (cells.shape[0] + cells.shape[2]) // ny, up.shape[1]), F32),
            jax.ShapeDtypeStruct(north.shape, F32),
        ),
        in_specs=[VMEM] * 6,
        out_specs=(VMEM, VMEM, VMEM),
        scratch_shapes=[
            pltpu.VMEM((chunks, n, rows, wide // chunks), BF),
            pltpu.VMEM((chunks, n, a_rows, wide // chunks), BF),
            pltpu.VMEM(east.shape, F32),
            dma(chunks, n), dma(chunks, n), dma(chunks, n), dma(chunks, n), dma(chunks, 2),
        ],
        compiler_params=pltpu.CompilerParams(collective_id=0, has_side_effects=True),
    )(field, gauss, cells, east, north, up)


def exchange_kernel(
    nx, ny, batches, per_c, w_ref, gt_ref, mask_ref, q_ref, py_ref,
    r_ref, fx_ref, fz_ref, pyo_ref,
    u_buf, q_in, q_all, y_in, z_in, z_own,
    us, ur, ul, qs, qr, ys, yr, zs, zr, gs, gr,
):
    gx, gy = lax.axis_index("gx"), lax.axis_index("gy")
    span = u_buf.shape[3]
    per = u_buf.shape[2]
    lanes = u_buf.shape[4]
    a_in = mask_ref.shape[0]
    deep = gt_ref.shape[1]
    x_rows = q_ref.shape[1] - z_in.shape[1]
    barrier = pltpu.get_barrier_semaphore()
    for d in range(1, ny):
        pl.semaphore_signal(barrier, inc=1, device_id=(gx, lax.rem(gy + d, ny)), device_id_type=MESH)
    for d in range(1, nx):
        pl.semaphore_signal(barrier, inc=1, device_id=(lax.rem(gx + d, nx), gy), device_id_type=MESH)
    pl.semaphore_wait(barrier, nx + ny - 2)

    small, ysmall, big = [], [], []
    for d in range(1, ny):
        to = lax.rem(gy + d, ny)
        small.append(remote(q_ref.at[to], q_in.at[d], qs.at[d], qr.at[d], (gx, to)))
    for d in range(1, nx):
        to = lax.rem(gx + d, nx)
        ysmall.append(remote(py_ref, y_in.at[d], ys.at[d], yr.at[d], (to, gy)))

    rows_b = per * span
    for b in range(batches):
        for d in range(1, ny + 1):
            to = lax.rem(gy + d, ny)
            for tile in range(lanes // 128):
                low = min(tile * 128 // per_c, a_in - 1)
                high = min((tile * 128 + 127) // per_c, a_in - 1)
                here = slice(tile * 128, tile * 128 + 128)
                weights = jnp.concatenate(
                    [gt_ref[to, :, here] * mask_ref[k : k + 1, here] for k in range(low, high + 1)], axis=0
                )
                left = w_ref[b * rows_b : (b + 1) * rows_b, low * deep : (high + 1) * deep]
                got = jnp.dot(left, weights, preferred_element_type=F32).astype(BF)
                u_buf[b, d - 1, :, :, here] = got.reshape(per, span, 128)
            target = r_ref.at[pl.ds(b * per, per), pl.ds(pl.multiple_of(gy * span, span), span), :]
            if d < ny:
                big.append(remote(u_buf.at[b, d - 1], target, us.at[b, d], ur.at[b, d], (gx, to)))
            else:
                own = pltpu.make_async_copy(u_buf.at[b, d - 1], target, ul.at[b])
                own.start()
                big.append(own)
        if b == 0:
            for copy in small:
                copy.wait()
            total = q_ref[gy]
            for d in range(1, ny):
                total = total + q_in[d]
            z_own[...] = total[x_rows:]
            zsmall = []
            for d in range(1, nx):
                to = lax.rem(gx + d, nx)
                zsmall.append(remote(z_own, z_in.at[d], zs.at[d], zr.at[d], (to, gy)))
            for copy in ysmall:
                copy.wait()
            y_in[0] = py_ref[...]
            y_total = jnp.zeros(py_ref.shape, F32)
            for g in range(nx):
                y_total = y_total + y_in[lax.rem(gx - g + nx, nx)]
            pyo_ref[...] = y_total
    for copy in zsmall:
        copy.wait()
    z_in[0] = z_own[...]
    z_total = jnp.zeros(z_own.shape, F32)
    for g in range(nx):
        z_total = z_total + z_in[lax.rem(gx - g + nx, nx)]
    q_all[gy, :x_rows] = total[:x_rows]
    q_all[gy, x_rows:] = z_total
    gathers = []
    for d in range(1, ny):
        to = lax.rem(gy + d, ny)
        gathers.append(remote(q_all.at[gy], q_all.at[gy], gs.at[d], gr.at[d], (gx, to)))
    for copy in gathers:
        copy.wait()
    z_rows = z_own.shape[0]
    for k in range(ny):
        fx_ref[k * x_rows : (k + 1) * x_rows] = q_all[k, :x_rows]
        fz_ref[k * z_rows : (k + 1) * z_rows] = q_all[k, x_rows:]
    for copy in big:
        copy.wait()


def line_kernel(
    nx, ny, batches, per_c, w_ref, gt_ref, mask_ref, q_ref, py_ref,
    r_ref, fx_ref, fz_ref, pyo_ref,
    w_in, u_buf, wt, q_in, q_all, y_in, z_in, z_own,
    ws, wr, us, ur, ul, qs, qr, ys, yr, zs, zr, gs, gr,
):
    gx, gy = lax.axis_index("gx"), lax.axis_index("gy")
    spot, core = gy // 2, gy % 2
    last = ny // 2 - 1
    middle = jnp.logical_and(spot > 0, spot < last)
    left_half = spot * 2 < last
    end = jnp.where(left_half, 0, last)
    near = jnp.where(left_half, 1, last - 1)
    _, _, _, per, span, lanes = u_buf.shape
    a_in = mask_ref.shape[0]
    deep = gt_ref.shape[1]
    x_rows = q_ref.shape[1] - z_in.shape[1]
    rows_b = per * span
    spots = (end, last - spot, last - end, spot)
    goals = (gy, 2 * spot + 1 - core, 2 * end, 2 * end + 1)
    barrier = pltpu.get_barrier_semaphore()
    for d in range(1, ny):
        pl.semaphore_signal(barrier, inc=1, device_id=(gx, lax.rem(gy + d, ny)), device_id_type=MESH)
    for d in range(1, nx):
        pl.semaphore_signal(barrier, inc=1, device_id=(lax.rem(gx + d, nx), gy), device_id_type=MESH)
    pl.semaphore_wait(barrier, nx + ny - 2)

    small, ysmall = [], []
    for d in range(1, ny):
        to = lax.rem(gy + d, ny)
        small.append(remote(q_ref.at[to], q_in.at[d], qs.at[d], qr.at[d], (gx, to)))
    for d in range(1, nx):
        to = lax.rem(gx + d, nx)
        ysmall.append(remote(py_ref, y_in.at[d], ys.at[d], yr.at[d], (to, gy)))

    def raw(src, slot, b, to_spot):
        return pltpu.make_async_remote_copy(
            src_ref=src, dst_ref=w_in.at[slot, b], send_sem=ws.at[slot, b], recv_sem=wr.at[slot, b],
            device_id=(gx, 2 * to_spot + core), device_id_type=MESH,
        )

    def rows_of(b):
        return w_ref.at[pl.ds(b * rows_b, rows_b), :]

    def place(b, origin):
        return r_ref.at[pl.ds(b * per, per), pl.ds(pl.multiple_of(origin * span, span), span), :]

    def block(kind, slot, b):
        source = 2 * spots[slot] + core
        if kind == 0:
            return pltpu.make_async_copy(u_buf.at[kind, slot, b], place(b, source), ul.at[slot, b])
        return pltpu.make_async_remote_copy(
            src_ref=u_buf.at[kind, slot, b], dst_ref=place(b, source),
            send_sem=us.at[kind, slot, b], recv_sem=ur.at[b, spots[slot], core],
            device_id=(gx, goals[kind]), device_id_type=MESH,
        )

    def arrived(b, at, side):
        pltpu.make_async_remote_copy(
            src_ref=u_buf.at[0, 0, b], dst_ref=place(b, 2 * at + side),
            send_sem=us.at[1, 0, b], recv_sem=ur.at[b, at, side],
            device_id=(gx, goals[1]), device_id_type=MESH,
        ).wait_recv()

    pieces, base = [], 0
    for tile in range(lanes // 128):
        low = min(tile * 128 // per_c, a_in - 1)
        high = min((tile * 128 + 127) // per_c, a_in - 1)
        pieces.append((tile, low, high, base))
        base += (high + 1 - low) * deep

    def weigh(kind):
        for tile, low, high, at in pieces:
            here = slice(tile * 128, tile * 128 + 128)
            for k in range(low, high + 1):
                wt[kind, at + (k - low) * deep : at + (k - low + 1) * deep] = (
                    gt_ref[goals[kind], :, here] * mask_ref[k : k + 1, here]
                )

    def mix(kind, slot, b, left):
        for tile, low, high, at in pieces:
            got = jnp.dot(
                left[:, low * deep : (high + 1) * deep],
                wt[kind, at : at + (high + 1 - low) * deep],
                preferred_element_type=F32,
            ).astype(BF)
            u_buf[kind, slot, b, :, :, tile * 128 : tile * 128 + 128] = got.reshape(per, span, 128)

    def own_blocks(kind):
        weigh(kind)
        for b in range(batches):
            mix(kind, 3, b, rows_of(b))
            block(kind, 3, b).start()

    @pl.when(middle)
    def _():
        for b in range(batches):
            raw(rows_of(b), 1, b, last - spot).start()
        for kind in (2, 3):
            own_blocks(kind)

    @pl.when(jnp.logical_not(middle))
    def _():
        for b in range(batches):
            raw(rows_of(b), 0, b, near).start()

    for kind in (1, 0):
        own_blocks(kind)

    for copy in small:
        copy.wait()
    total = q_ref[gy]
    for d in range(1, ny):
        total = total + q_in[d]
    z_own[...] = total[x_rows:]
    zsmall = []
    for d in range(1, nx):
        to = lax.rem(gx + d, nx)
        zsmall.append(remote(z_own, z_in.at[d], zs.at[d], zr.at[d], (to, gy)))
    for copy in ysmall:
        copy.wait()
    y_in[0] = py_ref[...]
    y_total = jnp.zeros(py_ref.shape, F32)
    for g in range(nx):
        y_total = y_total + y_in[lax.rem(gx - g + nx, nx)]
    pyo_ref[...] = y_total
    for copy in zsmall:
        copy.wait()
    z_in[0] = z_own[...]
    z_total = jnp.zeros(z_own.shape, F32)
    for g in range(nx):
        z_total = z_total + z_in[lax.rem(gx - g + nx, nx)]
    q_all[gy, :x_rows] = total[:x_rows]
    q_all[gy, x_rows:] = z_total
    gathers = []
    for d in range(1, ny):
        to = lax.rem(gy + d, ny)
        gathers.append(remote(q_all.at[gy], q_all.at[gy], gs.at[d], gr.at[d], (gx, to)))

    @pl.when(middle)
    def _():
        for b in range(batches):
            raw(rows_of(b), 0, b, near).wait_recv()
            raw(w_in.at[0, b], 2, b, last - spot).start()
            raw(rows_of(b), 1, b, last - spot).wait_recv()
            for kind, slot in ((2, 1), (3, 1), (1, 1), (1, 0), (0, 1), (0, 0)):
                mix(kind, slot, b, w_in.at[slot, b])
                block(kind, slot, b).start()
        for b in range(batches):
            raw(w_in.at[0, b], 2, b, last - spot).wait_recv()
            for kind in (2, 3, 1, 0):
                mix(kind, 2, b, w_in.at[2, b])
                block(kind, 2, b).start()
        for b in range(batches):
            raw(rows_of(b), 1, b, last - spot).wait_send()
            raw(w_in.at[0, b], 2, b, last - spot).wait_send()
            for slot in range(4):
                block(0, slot, b).wait()
                block(1, slot, b).wait_send()
                if slot:
                    block(2, slot, b).wait_send()
                    block(3, slot, b).wait_send()
                arrived(b, spots[slot], 1 - core)

    @pl.when(jnp.logical_not(middle))
    def _():
        for b in range(batches):
            raw(rows_of(b), 0, b, near).wait_send()
            block(0, 3, b).wait()
            block(1, 3, b).wait_send()
            arrived(b, spot, 1 - core)
            for d in range(1, ny // 2):
                for side in range(2):
                    arrived(b, lax.rem(spot + d, ny // 2), side)

    for copy in gathers:
        copy.wait()
    z_rows = z_own.shape[0]
    for k in range(ny):
        fx_ref[k * x_rows : (k + 1) * x_rows] = q_all[k, :x_rows]
        fz_ref[k * z_rows : (k + 1) * z_rows] = q_all[k, x_rows:]


def exchange(w, gt, mask, q, py, nx, ny, groups, span, per_c):
    lanes = gt.shape[2]
    deep = gt.shape[1]
    z_rows = deep // ny
    dma = lambda *shape: pltpu.SemaphoreType.DMA(shape)
    vm = pltpu.VMEM
    sums = [
        vm(q.shape, F32), vm(q.shape, F32), vm((nx,) + py.shape, F32),
        vm((nx, z_rows, q.shape[2]), F32), vm((z_rows, q.shape[2]), F32),
    ]
    sum_sems = [dma(ny), dma(ny), dma(nx), dma(nx), dma(nx), dma(nx), dma(ny), dma(ny)]
    if ny == 8 and groups % 4 == 0:
        batches = 4
        per = groups // batches
        total_k = sum(
            min((t * 128 + 127) // per_c, mask.shape[0] - 1) + 1 - t * 128 // per_c
            for t in range(lanes // 128)
        ) * deep
        body = functools.partial(line_kernel, nx, ny, batches, per_c)
        scratch = [
            vm((3, batches, per * span, w.shape[1]), BF),
            vm((4, 4, batches, per, span, lanes), BF),
            vm((4, total_k, 128), BF),
        ] + sums + [
            dma(3, batches), dma(3, batches), dma(4, 4, batches), dma(batches, ny // 2, 2),
            dma(4, batches),
        ] + sum_sems
    else:
        batches = 3 if groups % 3 == 0 else 1
        per = groups // batches
        body = functools.partial(exchange_kernel, nx, ny, batches, per_c)
        scratch = [vm((batches, ny, per, span, lanes), BF)] + sums + [
            dma(batches, ny), dma(batches, ny), dma(batches)
        ] + sum_sems
    return pl.pallas_call(
        body,
        out_shape=(
            jax.ShapeDtypeStruct((groups, ny * span, lanes), BF),
            jax.ShapeDtypeStruct((ny * q.shape[1] - deep, q.shape[2]), F32),
            jax.ShapeDtypeStruct((deep, q.shape[2]), F32),
            jax.ShapeDtypeStruct(py.shape, F32),
        ),
        in_specs=[VMEM] * 5,
        out_specs=(ANY, VMEM, VMEM, VMEM),
        scratch_shapes=scratch,
        compiler_params=pltpu.CompilerParams(collective_id=1, has_side_effects=True),
    )(w, gt, mask, q, py)


def flow_kernel(
    nx, ny, per_c, ft_ref, g_ref, gu_ref, sel_ref, mask_ref, east_ref, north_ref, up_ref,
    r_ref, fx_ref, fz_ref, fy_ref,
    f_buf, x_buf, y_buf, w_land, wf, w_own, w_in, u_buf, wt,
    q_buf, q_in, q_all, p_buf, y_in, z_in, z_own,
    s1, r1, l1, s2, r2, ws, wr, us, ur, ul, fs, qs, qr, ys, yr, zs, zr, gs, gr,
):
    gx, gy = lax.axis_index("gx"), lax.axis_index("gy")
    spot, core = gy // 2, gy % 2
    last = ny // 2 - 1
    middle = jnp.logical_and(spot > 0, spot < last)
    left_half = spot * 2 < last
    end = jnp.where(left_half, 0, last)
    near = jnp.where(left_half, 1, last - 1)
    spots = (end, last - spot, last - end, spot)
    goals = (gy, 2 * spot + 1 - core, 2 * end, 2 * end + 1)

    span, rows, deep = f_buf.shape
    steps, share = x_buf.shape[:2]
    _, _, _, groups, tall, lanes = u_buf.shape
    a_in = mask_ref.shape[0]
    a_rows = groups * a_in
    width = up_ref.shape[1]
    x_rows, z_rows = rows // ny, deep // ny

    load = pltpu.make_async_copy(ft_ref, f_buf, fs.at[0])
    load.start()
    barrier = pltpu.get_barrier_semaphore()
    for d in range(1, ny):
        pl.semaphore_signal(barrier, inc=1, device_id=(gx, lax.rem(gy + d, ny)), device_id_type=MESH)
    for d in range(1, nx):
        pl.semaphore_signal(barrier, inc=1, device_id=(lax.rem(gx + d, nx), gy), device_id_type=MESH)
    pl.semaphore_wait(barrier, nx + ny - 2)

    def send(src, dst, ssem, rsem, where):
        return pltpu.make_async_remote_copy(
            src_ref=src, dst_ref=dst, send_sem=ssem, recv_sem=rsem, device_id=where, device_id_type=MESH
        )

    def first(m, d):
        to = lax.rem(gx + d, nx)
        src = ft_ref.at[pl.ds(m * tall + to * share, share)]
        dst = x_buf.at[m, :, pl.ds(pl.multiple_of(gx * rows, rows), rows), :]
        if d == nx:
            return pltpu.make_async_copy(src, dst, l1.at[m])
        return send(src, dst, s1.at[m, d], r1.at[m, d], (to, gy))

    def second(m, d):
        to = lax.rem(gx + d, nx)
        return send(y_buf.at[m, d - 1], w_land.at[m, gx], s2.at[m, d], r2.at[m, d], (to, gy))

    def send_first(m):
        for d in range(1, nx + 1):
            first(m, d).start()

    def mix_first(m):
        first(m, nx).wait()
        for d in range(1, nx):
            first(m, d).wait_recv()
        block = jnp.concatenate([x_buf[m, j] for j in range(share)], axis=1)
        for d in range(1, nx + 1):
            to = lax.rem(gx + d, nx)
            got = jnp.dot(g_ref[to], block, preferred_element_type=F32).astype(BF)
            if d < nx:
                y_buf[m, d - 1] = got
                second(m, d).start()
            else:
                w_land[m, gx] = got

    def raw(src, slot, m, to_spot):
        return send(src, w_in.at[slot, m], ws.at[slot, m], wr.at[slot, m], (gx, 2 * to_spot + core))

    def place(m, origin):
        return r_ref.at[:, pl.ds(pl.multiple_of(origin * span + m * tall, tall), tall), :]

    def block(kind, slot, m):
        source = 2 * spots[slot] + core
        if kind == 0:
            return pltpu.make_async_copy(u_buf.at[kind, slot, m], place(m, source), ul.at[slot, m])
        return send(
            u_buf.at[kind, slot, m], place(m, source), us.at[kind, slot, m],
            ur.at[m, spots[slot], core], (gx, goals[kind]),
        )

    def arrived(m, at, side):
        send(
            u_buf.at[0, 0, m], place(m, 2 * at + side), us.at[1, 0, m], ur.at[m, at, side], (gx, goals[1])
        ).wait_recv()

    pieces, base = [], 0
    for tile in range(lanes // 128):
        low = min(tile * 128 // per_c, a_in - 1)
        high = min((tile * 128 + 127) // per_c, a_in - 1)
        pieces.append((tile, low, high, base))
        base += (high + 1 - low) * deep

    def weigh(kind):
        mine = gu_ref[pl.ds(pl.multiple_of(goals[kind] * per_c, per_c), per_c), :]
        spread = lax.dot_general(
            mine, sel_ref[...], (((0,), (0,)), ((), ())), preferred_element_type=F32
        )
        for tile, low, high, at in pieces:
            here = slice(tile * 128, tile * 128 + 128)
            for k in range(low, high + 1):
                wt[kind, at + (k - low) * deep : at + (k - low + 1) * deep] = (
                    spread[:, here] * mask_ref[k : k + 1, here]
                ).astype(BF)

    def mix(kind, slot, m, left):
        for tile, low, high, at in pieces:
            got = jnp.dot(
                left[:, low * deep : (high + 1) * deep],
                wt[kind, at : at + (high + 1 - low) * deep],
                preferred_element_type=F32,
            )
            u_buf[kind, slot, m, :, :, tile * 128 : tile * 128 + 128] = (
                got.reshape(groups, tall, 128).astype(BF)
            )
        block(kind, slot, m).start()

    def settle(m):
        for d in range(1, nx):
            second(m, d).wait_recv()
        for y in range(tall):
            at = (y % share) * deep
            wf[pl.ds(y, a_rows, stride=tall), :] = w_land[m, y // share, :, at : at + deep].astype(F32)
        for k in range(a_in):
            part = jnp.concatenate(
                [wf[(g * a_in + k) * tall : (g * a_in + k + 1) * tall, :] for g in range(groups)], axis=0
            )
            w_own[m, :, k * deep : (k + 1) * deep] = part.astype(BF)

    def sketch():
        step = 16 if span % 16 == 0 else span
        along_x = east_ref[...].astype(F32)[None]
        part_x = jnp.zeros((rows, width), F32)
        part_z = jnp.zeros((deep, width), F32)
        for c in range(0, span, step):
            cells = f_buf[c : c + step].reshape(step * rows, deep)
            along_y = north_ref[c : c + step].astype(F32)[:, None, :]
            weighted = jnp.dot(cells, up_ref[...], preferred_element_type=F32).reshape(step, rows, width)
            p_buf[c : c + step] = jnp.sum(weighted * along_x, axis=1)
            part_x = part_x + jnp.sum(weighted * along_y, axis=0)
            khatri = (along_x * along_y).astype(BF).reshape(step * rows, width)
            part_z = part_z + lax.dot_general(
                cells, khatri, (((0,), (0,)), ((), ())), preferred_element_type=F32
            )
        for k in range(ny):
            q_buf[k, :x_rows] = part_x[k * x_rows : (k + 1) * x_rows]
            q_buf[k, x_rows:] = part_z[k * z_rows : (k + 1) * z_rows]

    def small(d):
        to = lax.rem(gy + d, ny)
        return send(q_buf.at[to], q_in.at[d], qs.at[d], qr.at[d], (gx, to))

    def small_y(d):
        to = lax.rem(gx + d, nx)
        return send(p_buf, y_in.at[d], ys.at[d], yr.at[d], (to, gy))

    def small_z(d):
        to = lax.rem(gx + d, nx)
        return send(z_own, z_in.at[d], zs.at[d], zr.at[d], (to, gy))

    def gather(d):
        to = lax.rem(gy + d, ny)
        return send(q_all.at[gy], q_all.at[gy], gs.at[d], gr.at[d], (gx, to))

    def gathered(d):
        source = lax.rem(gy - d + ny, ny)
        return send(q_all.at[source], q_all.at[source], gs.at[d], gr.at[d], (gx, source))

    send_first(0)
    send_first(1)
    load.wait()
    sketch()
    for d in range(1, ny):
        small(d).start()
    for d in range(1, nx):
        small_y(d).start()
    mix_first(0)
    send_first(2)
    for kind in range(4):
        weigh(kind)

    def stage(s, carry):
        @pl.when(s + 1 < steps)
        def _():
            mix_first(s + 1)

        @pl.when(s + 3 < steps)
        def _():
            send_first(s + 3)

        @pl.when(s < steps)
        def _():
            settle(s)

        @pl.when(jnp.logical_and(s < steps, middle))
        def _():
            raw(w_own.at[s], 1, s, last - spot).start()
            for kind in (2, 3):
                mix(kind, 3, s, w_own.at[s])

        @pl.when(jnp.logical_and(s < steps, jnp.logical_not(middle)))
        def _():
            raw(w_own.at[s], 0, s, near).start()

        @pl.when(s < steps)
        def _():
            for kind in (1, 0):
                mix(kind, 3, s, w_own.at[s])

        @pl.when(jnp.logical_and(jnp.logical_and(s >= 1, s < steps + 1), middle))
        def _():
            m = s - 1
            raw(w_own.at[m], 0, m, near).wait_recv()
            raw(w_in.at[0, m], 2, m, last - spot).start()
            raw(w_own.at[m], 1, m, last - spot).wait_recv()
            for kind, slot in ((2, 1), (3, 1), (1, 1), (0, 1), (1, 0), (0, 0)):
                mix(kind, slot, m, w_in.at[slot, m])

        @pl.when(jnp.logical_and(s >= 2, middle))
        def _():
            m = s - 2
            raw(w_in.at[0, m], 2, m, last - spot).wait_recv()
            for kind in (2, 3, 1, 0):
                mix(kind, 2, m, w_in.at[2, m])

        @pl.when(s == 1)
        def _():
            for d in range(1, ny):
                small(d).wait()
            total = q_buf[gy]
            for d in range(1, ny):
                total = total + q_in[d]
            q_all[gy] = total
            z_own[...] = total[x_rows:]
            for d in range(1, nx):
                small_z(d).start()

        @pl.when(s == 3)
        def _():
            for d in range(1, nx):
                small_y(d).wait()
                small_z(d).wait()
            y_in[0] = p_buf[...]
            z_in[0] = z_own[...]
            y_total = jnp.zeros(p_buf.shape, F32)
            z_total = jnp.zeros(z_own.shape, F32)
            for g in range(nx):
                y_total = y_total + y_in[lax.rem(gx - g + nx, nx)]
                z_total = z_total + z_in[lax.rem(gx - g + nx, nx)]
            fy_ref[...] = y_total
            q_all[gy, x_rows:] = z_total
            for d in range(1, ny):
                gather(d).start()

        return carry

    lax.fori_loop(0, steps + 2, stage, 0)

    for d in range(1, ny):
        gather(d).wait_send()
        gathered(d).wait_recv()
    for k in range(ny):
        fx_ref[k * x_rows : (k + 1) * x_rows] = q_all[k, :x_rows]
        fz_ref[k * z_rows : (k + 1) * z_rows] = q_all[k, x_rows:]

    def close(m, carry):
        for d in range(1, nx):
            first(m, d).wait_send()
            second(m, d).wait_send()
        block(0, 3, m).wait()
        block(1, 3, m).wait_send()
        arrived(m, spot, 1 - core)

        @pl.when(middle)
        def _():
            raw(w_own.at[m], 1, m, last - spot).wait_send()
            raw(w_in.at[0, m], 2, m, last - spot).wait_send()
            block(2, 3, m).wait_send()
            block(3, 3, m).wait_send()
            for slot in range(3):
                block(0, slot, m).wait()
                block(1, slot, m).wait_send()
                if slot:
                    block(2, slot, m).wait_send()
                    block(3, slot, m).wait_send()
                arrived(m, spots[slot], 1 - core)

        @pl.when(jnp.logical_not(middle))
        def _():
            raw(w_own.at[m], 0, m, near).wait_send()
            for d in range(1, ny // 2):
                for side in range(2):
                    arrived(m, lax.rem(spot + d, ny // 2), side)

        return carry

    lax.fori_loop(0, steps, close, 0)


def flow(field, gauss_east, gauss_up, east, north, up, nx, ny, a_in, lanes):
    rows, span, deep = field.shape
    a_rows = gauss_east.shape[0] // nx
    per_c = gauss_up.shape[0] // ny
    groups = a_rows // a_in
    tall = 8
    steps, share = span // tall, tall // nx
    width = up.shape[1]
    x_rows, z_rows = rows // ny, deep // ny
    lane = np.arange(lanes)
    used = lane < a_in * per_c
    sel = np.logical_and(lane[None] % per_c == np.arange(per_c)[:, None], used[None]).astype(np.float32)
    mask = (lane[None] // per_c == np.arange(a_in)[:, None]).astype(np.float32)
    total_k = sum(
        min((t * 128 + 127) // per_c, a_in - 1) + 1 - min(t * 128 // per_c, a_in - 1)
        for t in range(lanes // 128)
    ) * deep
    dma = lambda *shape: pltpu.SemaphoreType.DMA(shape)
    vm = pltpu.VMEM
    q_shape = (ny, x_rows + z_rows, width)
    scratch = [
        vm((span, rows, deep), BF),
        vm((steps, share, nx * rows, deep), BF),
        vm((steps, nx - 1, a_rows, share * deep), BF),
        vm((steps, nx, a_rows, share * deep), BF),
        vm((a_rows * tall, deep), F32),
        vm((steps, groups * tall, a_in * deep), BF),
        vm((3, steps, groups * tall, a_in * deep), BF),
        vm((4, 4, steps, groups, tall, lanes), BF),
        vm((4, total_k, 128), BF),
        vm(q_shape, F32), vm(q_shape, F32), vm(q_shape, F32),
        vm((span, width), F32), vm((nx, span, width), F32),
        vm((nx, z_rows, width), F32), vm((z_rows, width), F32),
        dma(steps, nx), dma(steps, nx), dma(steps), dma(steps, nx), dma(steps, nx),
        dma(3, steps), dma(3, steps), dma(4, 4, steps), dma(steps, ny // 2, 2), dma(4, steps), dma(1),
        dma(ny), dma(ny), dma(nx), dma(nx), dma(nx), dma(nx), dma(ny), dma(ny),
    ]
    return pl.pallas_call(
        functools.partial(flow_kernel, nx, ny, per_c),
        out_shape=(
            jax.ShapeDtypeStruct((groups, ny * span, lanes), BF),
            jax.ShapeDtypeStruct((rows, width), F32),
            jax.ShapeDtypeStruct((deep, width), F32),
            jax.ShapeDtypeStruct((span, width), F32),
        ),
        in_specs=[ANY] + [VMEM] * 7,
        out_specs=(ANY, VMEM, VMEM, VMEM),
        scratch_shapes=scratch,
        compiler_params=pltpu.CompilerParams(collective_id=2, has_side_effects=True),
    )(
        field.transpose(1, 0, 2), gauss_east.reshape(nx, a_rows, -1), gauss_up,
        jnp.asarray(sel, BF), jnp.asarray(mask, F32), east, north, up,
    )


def mix_y_kernel(r_ref, g_ref, o_ref):
    for k in range(r_ref.shape[0]):
        o_ref[k] = lax.dot_general(
            r_ref[k], g_ref[...], (((0,), (1,)), ((), ())), preferred_element_type=F32
        )


def mix_y(r, g):
    groups, deep, lanes = r.shape
    out = g.shape[0]
    take = 2 if groups % 2 == 0 else 1
    return pl.pallas_call(
        mix_y_kernel,
        grid=(groups // take,),
        out_shape=jax.ShapeDtypeStruct((groups, lanes, out), F32),
        in_specs=[
            pl.BlockSpec((take, deep, lanes), lambda i: (i, 0, 0)),
            pl.BlockSpec((out, deep), lambda i: (0, 0)),
        ],
        out_specs=pl.BlockSpec((take, lanes, out), lambda i: (i, 0, 0)),
    )(r, g)


def per_device(
    nx, ny,
    thermal_field,
    probe_range_east,
    probe_range_north,
    probe_range_upward,
    gauss_kernel_east,
    gauss_kernel_north,
    gauss_kernel_upward,
):
    rows, span, deep = thermal_field.shape
    a_rows = gauss_kernel_east.shape[0] // nx
    per_c = gauss_kernel_upward.shape[0] // ny
    a_in = 8 if a_rows % 8 == 0 and 8 * per_c % 128 == 0 else a_rows
    groups = a_rows // a_in
    used = a_in * per_c
    lanes = -(-used // 128) * 128

    if ny == 8 and 8 % nx == 0 and span % 8 == 0 and span // 8 > 2 and a_in % 8 == 0 and per_c % 16 == 0:
        r, factor_x, factor_z, factor_y = flow(
            thermal_field, gauss_kernel_east, gauss_kernel_upward,
            probe_range_east, probe_range_north, probe_range_upward, nx, ny, a_in, lanes,
        )
    else:
        w, q, part_y = mix_x(
            thermal_field.reshape(rows, span * deep),
            gauss_kernel_east.reshape(nx, a_rows, -1),
            nx,
            a_rows,
            thermal_field,
            probe_range_east,
            probe_range_north,
            probe_range_upward,
            ny,
        )
        w = w.reshape(groups, a_in, span, deep).transpose(0, 2, 1, 3).reshape(groups * span, a_in * deep)

        gt = gauss_kernel_upward.reshape(ny, per_c, deep).transpose(0, 2, 1)
        gt = jnp.pad(jnp.tile(gt, (1, 1, a_in)), ((0, 0), (0, 0), (0, lanes - used)))
        mask = (
            lax.broadcasted_iota(jnp.int32, (a_in, lanes), 1) // per_c
            == lax.broadcasted_iota(jnp.int32, (a_in, lanes), 0)
        ).astype(BF)
        r, factor_x, factor_z, factor_y = exchange(w, gt, mask, q, part_y, nx, ny, groups, span, per_c)

    core = mix_y(r, gauss_kernel_north)
    core = core[:, :used].reshape(a_rows, per_c, -1).transpose(0, 2, 1)
    return (factor_x, factor_y, factor_z, core)


def solution(mesh):
    in_specs = (P("gx", "gy", None), P("gx", None), P("gy", None), P(), P(), P(), P())
    out_specs = (P("gx", None), P("gy", None), P(), P("gx", None, "gy"))
    body = functools.partial(per_device, mesh.shape["gx"], mesh.shape["gy"])
    return jax.shard_map(
        body, mesh=mesh, in_specs=in_specs, out_specs=out_specs, check_vma=False
    )
```

```python
import functools

import jax
import jax.numpy as jnp
import numpy as np
from jax import lax
from jax.experimental import pallas as pl
from jax.experimental.pallas import tpu as pltpu
from jax.sharding import PartitionSpec as P

MESH = pl.DeviceIdType.MESH
VMEM = pl.BlockSpec(memory_space=pltpu.VMEM)
ANY = pl.BlockSpec(memory_space=pl.ANY)
BF = jnp.bfloat16
F32 = jnp.float32


def remote(src, dst, send, recv, where):
    copy = pltpu.make_async_remote_copy(
        src_ref=src, dst_ref=dst, send_sem=send, recv_sem=recv, device_id=where, device_id_type=MESH
    )
    copy.start()
    return copy


def sketch_parts(f_ref, east_ref, north_ref, up_ref, q_ref, py_ref, px_buf):
    rows, span, deep = f_ref.shape
    width = up_ref.shape[1]
    step = 16 if rows % 16 == 0 else rows
    along_y = north_ref[...].astype(F32)
    part_y = jnp.zeros((span, width), F32)
    part_z = jnp.zeros((deep, width), F32)
    for c in range(0, rows, step):
        cells = f_ref[c : c + step].reshape(step * span, deep)
        along_x = east_ref[c : c + step].astype(F32)
        weighted = jnp.dot(cells, up_ref[...], preferred_element_type=F32).reshape(step, span, width)
        px_buf[c : c + step] = jnp.sum(weighted * along_y[None, :, :], axis=1)
        part_y = part_y + jnp.sum(weighted * along_x[:, None, :], axis=0)
        khatri = (along_x[:, None, :] * along_y[None, :, :]).astype(BF).reshape(step * span, width)
        part_z = part_z + lax.dot_general(
            cells, khatri, (((0,), (0,)), ((), ())), preferred_element_type=F32
        )
    py_ref[...] = part_y
    ny = q_ref.shape[0]
    x_rows, z_rows = rows // ny, deep // ny
    for k in range(ny):
        q_ref[k, :x_rows] = px_buf[k * x_rows : (k + 1) * x_rows]
        q_ref[k, x_rows:] = part_z[k * z_rows : (k + 1) * z_rows]


def mix_x_kernel(
    n, chunks, t_ref, g_ref, f_ref, east_ref, north_ref, up_ref, w_ref, q_ref, py_ref,
    x_buf, y_buf, px_buf, s1, r1, s2, r2, ls,
):
    gx, gy = lax.axis_index("gx"), lax.axis_index("gy")
    rows = t_ref.shape[0]
    a_rows = y_buf.shape[2]
    wide = t_ref.shape[1] // n
    part = wide // chunks
    barrier = pltpu.get_barrier_semaphore()
    for d in range(1, n):
        pl.semaphore_signal(barrier, inc=1, device_id=(lax.rem(gx + d, n), gy), device_id_type=MESH)
    pl.semaphore_wait(barrier, n - 1)

    first, second, local = [], [], []
    for m in range(chunks):
        for d in range(1, n):
            to = lax.rem(gx + d, n)
            lanes = pl.ds(pl.multiple_of(to * wide + m * part, 128), part)
            first.append(
                remote(t_ref.at[:, lanes], x_buf.at[m, gx], s1.at[m, d], r1.at[m, d], (to, gy))
            )
        lanes = pl.ds(pl.multiple_of(gx * wide + m * part, 128), part)
        own = pltpu.make_async_copy(t_ref.at[:, lanes], x_buf.at[m, gx], ls.at[m, 0])
        own.start()
        local.append(own)
    sketch_parts(f_ref, east_ref, north_ref, up_ref, q_ref, py_ref, px_buf)
    for m in range(chunks):
        local[m].wait()
        for d in range(1, n):
            first[m * (n - 1) + d - 1].wait()
        block = x_buf[m].reshape(n * rows, part)
        lanes = pl.ds(pl.multiple_of(gx * wide + m * part, 128), part)
        for d in range(1, n + 1):
            to = lax.rem(gx + d, n)
            y_buf[m, d - 1] = jnp.dot(g_ref[to], block, preferred_element_type=F32).astype(BF)
            if d < n:
                second.append(
                    remote(
                        y_buf.at[m, d - 1], w_ref.at[:, lanes], s2.at[m, d], r2.at[m, d], (to, gy)
                    )
                )
            else:
                own = pltpu.make_async_copy(y_buf.at[m, d - 1], w_ref.at[:, lanes], ls.at[m, 1])
                own.start()
                second.append(own)
    for copy in second:
        copy.wait()


def mix_x(field, gauss, n, a_rows, cells, east, north, up, ny):
    rows, lanes = field.shape
    wide = lanes // n
    chunks = 3 if wide % 384 == 0 else 1
    dma = lambda *shape: pltpu.SemaphoreType.DMA(shape)
    return pl.pallas_call(
        functools.partial(mix_x_kernel, n, chunks),
        out_shape=(
            jax.ShapeDtypeStruct((a_rows, lanes), BF),
            jax.ShapeDtypeStruct((ny, (cells.shape[0] + cells.shape[2]) // ny, up.shape[1]), F32),
            jax.ShapeDtypeStruct(north.shape, F32),
        ),
        in_specs=[VMEM] * 6,
        out_specs=(VMEM, VMEM, VMEM),
        scratch_shapes=[
            pltpu.VMEM((chunks, n, rows, wide // chunks), BF),
            pltpu.VMEM((chunks, n, a_rows, wide // chunks), BF),
            pltpu.VMEM(east.shape, F32),
            dma(chunks, n), dma(chunks, n), dma(chunks, n), dma(chunks, n), dma(chunks, 2),
        ],
        compiler_params=pltpu.CompilerParams(collective_id=0, has_side_effects=True),
    )(field, gauss, cells, east, north, up)


def exchange_kernel(
    nx, ny, batches, per_c, w_ref, gt_ref, mask_ref, q_ref, py_ref,
    r_ref, fx_ref, fz_ref, pyo_ref,
    u_buf, q_in, q_all, y_in, z_in, z_own,
    us, ur, ul, qs, qr, ys, yr, zs, zr, gs, gr,
):
    gx, gy = lax.axis_index("gx"), lax.axis_index("gy")
    span = u_buf.shape[3]
    per = u_buf.shape[2]
    lanes = u_buf.shape[4]
    a_in = mask_ref.shape[0]
    deep = gt_ref.shape[1]
    x_rows = q_ref.shape[1] - z_in.shape[1]
    barrier = pltpu.get_barrier_semaphore()
    for d in range(1, ny):
        pl.semaphore_signal(barrier, inc=1, device_id=(gx, lax.rem(gy + d, ny)), device_id_type=MESH)
    for d in range(1, nx):
        pl.semaphore_signal(barrier, inc=1, device_id=(lax.rem(gx + d, nx), gy), device_id_type=MESH)
    pl.semaphore_wait(barrier, nx + ny - 2)

    small, ysmall, big = [], [], []
    for d in range(1, ny):
        to = lax.rem(gy + d, ny)
        small.append(remote(q_ref.at[to], q_in.at[d], qs.at[d], qr.at[d], (gx, to)))
    for d in range(1, nx):
        to = lax.rem(gx + d, nx)
        ysmall.append(remote(py_ref, y_in.at[d], ys.at[d], yr.at[d], (to, gy)))

    rows_b = per * span
    for b in range(batches):
        for d in range(1, ny + 1):
            to = lax.rem(gy + d, ny)
            for tile in range(lanes // 128):
                low = min(tile * 128 // per_c, a_in - 1)
                high = min((tile * 128 + 127) // per_c, a_in - 1)
                here = slice(tile * 128, tile * 128 + 128)
                weights = jnp.concatenate(
                    [gt_ref[to, :, here] * mask_ref[k : k + 1, here] for k in range(low, high + 1)], axis=0
                )
                left = w_ref[b * rows_b : (b + 1) * rows_b, low * deep : (high + 1) * deep]
                got = jnp.dot(left, weights, preferred_element_type=F32).astype(BF)
                u_buf[b, d - 1, :, :, here] = got.reshape(per, span, 128)
            target = r_ref.at[pl.ds(b * per, per), pl.ds(pl.multiple_of(gy * span, span), span), :]
            if d < ny:
                big.append(remote(u_buf.at[b, d - 1], target, us.at[b, d], ur.at[b, d], (gx, to)))
            else:
                own = pltpu.make_async_copy(u_buf.at[b, d - 1], target, ul.at[b])
                own.start()
                big.append(own)
        if b == 0:
            for copy in small:
                copy.wait()
            total = q_ref[gy]
            for d in range(1, ny):
                total = total + q_in[d]
            z_own[...] = total[x_rows:]
            zsmall = []
            for d in range(1, nx):
                to = lax.rem(gx + d, nx)
                zsmall.append(remote(z_own, z_in.at[d], zs.at[d], zr.at[d], (to, gy)))
            for copy in ysmall:
                copy.wait()
            y_in[0] = py_ref[...]
            y_total = jnp.zeros(py_ref.shape, F32)
            for g in range(nx):
                y_total = y_total + y_in[lax.rem(gx - g + nx, nx)]
            pyo_ref[...] = y_total
    for copy in zsmall:
        copy.wait()
    z_in[0] = z_own[...]
    z_total = jnp.zeros(z_own.shape, F32)
    for g in range(nx):
        z_total = z_total + z_in[lax.rem(gx - g + nx, nx)]
    q_all[gy, :x_rows] = total[:x_rows]
    q_all[gy, x_rows:] = z_total
    gathers = []
    for d in range(1, ny):
        to = lax.rem(gy + d, ny)
        gathers.append(remote(q_all.at[gy], q_all.at[gy], gs.at[d], gr.at[d], (gx, to)))
    for copy in gathers:
        copy.wait()
    z_rows = z_own.shape[0]
    for k in range(ny):
        fx_ref[k * x_rows : (k + 1) * x_rows] = q_all[k, :x_rows]
        fz_ref[k * z_rows : (k + 1) * z_rows] = q_all[k, x_rows:]
    for copy in big:
        copy.wait()


def line_kernel(
    nx, ny, batches, per_c, w_ref, gt_ref, mask_ref, q_ref, py_ref,
    r_ref, fx_ref, fz_ref, pyo_ref,
    w_in, u_buf, wt, q_in, q_all, y_in, z_in, z_own,
    ws, wr, us, ur, ul, qs, qr, ys, yr, zs, zr, gs, gr,
):
    gx, gy = lax.axis_index("gx"), lax.axis_index("gy")
    spot, core = gy // 2, gy % 2
    last = ny // 2 - 1
    middle = jnp.logical_and(spot > 0, spot < last)
    left_half = spot * 2 < last
    end = jnp.where(left_half, 0, last)
    near = jnp.where(left_half, 1, last - 1)
    _, _, _, per, span, lanes = u_buf.shape
    a_in = mask_ref.shape[0]
    deep = gt_ref.shape[1]
    x_rows = q_ref.shape[1] - z_in.shape[1]
    rows_b = per * span
    spots = (end, last - spot, last - end, spot)
    goals = (gy, 2 * spot + 1 - core, 2 * end, 2 * end + 1)
    barrier = pltpu.get_barrier_semaphore()
    for d in range(1, ny):
        pl.semaphore_signal(barrier, inc=1, device_id=(gx, lax.rem(gy + d, ny)), device_id_type=MESH)
    for d in range(1, nx):
        pl.semaphore_signal(barrier, inc=1, device_id=(lax.rem(gx + d, nx), gy), device_id_type=MESH)
    pl.semaphore_wait(barrier, nx + ny - 2)

    small, ysmall = [], []
    for d in range(1, ny):
        to = lax.rem(gy + d, ny)
        small.append(remote(q_ref.at[to], q_in.at[d], qs.at[d], qr.at[d], (gx, to)))
    for d in range(1, nx):
        to = lax.rem(gx + d, nx)
        ysmall.append(remote(py_ref, y_in.at[d], ys.at[d], yr.at[d], (to, gy)))

    def raw(src, slot, b, to_spot):
        return pltpu.make_async_remote_copy(
            src_ref=src, dst_ref=w_in.at[slot, b], send_sem=ws.at[slot, b], recv_sem=wr.at[slot, b],
            device_id=(gx, 2 * to_spot + core), device_id_type=MESH,
        )

    def rows_of(b):
        return w_ref.at[pl.ds(b * rows_b, rows_b), :]

    def place(b, origin):
        return r_ref.at[pl.ds(b * per, per), pl.ds(pl.multiple_of(origin * span, span), span), :]

    def block(kind, slot, b):
        source = 2 * spots[slot] + core
        if kind == 0:
            return pltpu.make_async_copy(u_buf.at[kind, slot, b], place(b, source), ul.at[slot, b])
        return pltpu.make_async_remote_copy(
            src_ref=u_buf.at[kind, slot, b], dst_ref=place(b, source),
            send_sem=us.at[kind, slot, b], recv_sem=ur.at[b, spots[slot], core],
            device_id=(gx, goals[kind]), device_id_type=MESH,
        )

    def arrived(b, at, side):
        pltpu.make_async_remote_copy(
            src_ref=u_buf.at[0, 0, b], dst_ref=place(b, 2 * at + side),
            send_sem=us.at[1, 0, b], recv_sem=ur.at[b, at, side],
            device_id=(gx, goals[1]), device_id_type=MESH,
        ).wait_recv()

    pieces, base = [], 0
    for tile in range(lanes // 128):
        low = min(tile * 128 // per_c, a_in - 1)
        high = min((tile * 128 + 127) // per_c, a_in - 1)
        pieces.append((tile, low, high, base))
        base += (high + 1 - low) * deep

    def weigh(kind):
        for tile, low, high, at in pieces:
            here = slice(tile * 128, tile * 128 + 128)
            for k in range(low, high + 1):
                wt[kind, at + (k - low) * deep : at + (k - low + 1) * deep] = (
                    gt_ref[goals[kind], :, here] * mask_ref[k : k + 1, here]
                )

    def mix(kind, slot, b, left):
        for tile, low, high, at in pieces:
            got = jnp.dot(
                left[:, low * deep : (high + 1) * deep],
                wt[kind, at : at + (high + 1 - low) * deep],
                preferred_element_type=F32,
            ).astype(BF)
            u_buf[kind, slot, b, :, :, tile * 128 : tile * 128 + 128] = got.reshape(per, span, 128)

    def own_blocks(kind):
        weigh(kind)
        for b in range(batches):
            mix(kind, 3, b, rows_of(b))
            block(kind, 3, b).start()

    @pl.when(middle)
    def _():
        for b in range(batches):
            raw(rows_of(b), 1, b, last - spot).start()
        for kind in (2, 3):
            own_blocks(kind)

    @pl.when(jnp.logical_not(middle))
    def _():
        for b in range(batches):
            raw(rows_of(b), 0, b, near).start()

    for kind in (1, 0):
        own_blocks(kind)

    for copy in small:
        copy.wait()
    total = q_ref[gy]
    for d in range(1, ny):
        total = total + q_in[d]
    z_own[...] = total[x_rows:]
    zsmall = []
    for d in range(1, nx):
        to = lax.rem(gx + d, nx)
        zsmall.append(remote(z_own, z_in.at[d], zs.at[d], zr.at[d], (to, gy)))
    for copy in ysmall:
        copy.wait()
    y_in[0] = py_ref[...]
    y_total = jnp.zeros(py_ref.shape, F32)
    for g in range(nx):
        y_total = y_total + y_in[lax.rem(gx - g + nx, nx)]
    pyo_ref[...] = y_total
    for copy in zsmall:
        copy.wait()
    z_in[0] = z_own[...]
    z_total = jnp.zeros(z_own.shape, F32)
    for g in range(nx):
        z_total = z_total + z_in[lax.rem(gx - g + nx, nx)]
    q_all[gy, :x_rows] = total[:x_rows]
    q_all[gy, x_rows:] = z_total
    gathers = []
    for d in range(1, ny):
        to = lax.rem(gy + d, ny)
        gathers.append(remote(q_all.at[gy], q_all.at[gy], gs.at[d], gr.at[d], (gx, to)))

    @pl.when(middle)
    def _():
        for b in range(batches):
            raw(rows_of(b), 0, b, near).wait_recv()
            raw(w_in.at[0, b], 2, b, last - spot).start()
            raw(rows_of(b), 1, b, last - spot).wait_recv()
            for kind, slot in ((2, 1), (3, 1), (1, 1), (1, 0), (0, 1), (0, 0)):
                mix(kind, slot, b, w_in.at[slot, b])
                block(kind, slot, b).start()
        for b in range(batches):
            raw(w_in.at[0, b], 2, b, last - spot).wait_recv()
            for kind in (2, 3, 1, 0):
                mix(kind, 2, b, w_in.at[2, b])
                block(kind, 2, b).start()
        for b in range(batches):
            raw(rows_of(b), 1, b, last - spot).wait_send()
            raw(w_in.at[0, b], 2, b, last - spot).wait_send()
            for slot in range(4):
                block(0, slot, b).wait()
                block(1, slot, b).wait_send()
                if slot:
                    block(2, slot, b).wait_send()
                    block(3, slot, b).wait_send()
                arrived(b, spots[slot], 1 - core)

    @pl.when(jnp.logical_not(middle))
    def _():
        for b in range(batches):
            raw(rows_of(b), 0, b, near).wait_send()
            block(0, 3, b).wait()
            block(1, 3, b).wait_send()
            arrived(b, spot, 1 - core)
            for d in range(1, ny // 2):
                for side in range(2):
                    arrived(b, lax.rem(spot + d, ny // 2), side)

    for copy in gathers:
        copy.wait()
    z_rows = z_own.shape[0]
    for k in range(ny):
        fx_ref[k * x_rows : (k + 1) * x_rows] = q_all[k, :x_rows]
        fz_ref[k * z_rows : (k + 1) * z_rows] = q_all[k, x_rows:]


def exchange(w, gt, mask, q, py, nx, ny, groups, span, per_c):
    lanes = gt.shape[2]
    deep = gt.shape[1]
    z_rows = deep // ny
    dma = lambda *shape: pltpu.SemaphoreType.DMA(shape)
    vm = pltpu.VMEM
    sums = [
        vm(q.shape, F32), vm(q.shape, F32), vm((nx,) + py.shape, F32),
        vm((nx, z_rows, q.shape[2]), F32), vm((z_rows, q.shape[2]), F32),
    ]
    sum_sems = [dma(ny), dma(ny), dma(nx), dma(nx), dma(nx), dma(nx), dma(ny), dma(ny)]
    if ny == 8 and groups % 4 == 0:
        batches = 4
        per = groups // batches
        total_k = sum(
            min((t * 128 + 127) // per_c, mask.shape[0] - 1) + 1 - t * 128 // per_c
            for t in range(lanes // 128)
        ) * deep
        body = functools.partial(line_kernel, nx, ny, batches, per_c)
        scratch = [
            vm((3, batches, per * span, w.shape[1]), BF),
            vm((4, 4, batches, per, span, lanes), BF),
            vm((4, total_k, 128), BF),
        ] + sums + [
            dma(3, batches), dma(3, batches), dma(4, 4, batches), dma(batches, ny // 2, 2),
            dma(4, batches),
        ] + sum_sems
    else:
        batches = 3 if groups % 3 == 0 else 1
        per = groups // batches
        body = functools.partial(exchange_kernel, nx, ny, batches, per_c)
        scratch = [vm((batches, ny, per, span, lanes), BF)] + sums + [
            dma(batches, ny), dma(batches, ny), dma(batches)
        ] + sum_sems
    return pl.pallas_call(
        body,
        out_shape=(
            jax.ShapeDtypeStruct((groups, ny * span, lanes), BF),
            jax.ShapeDtypeStruct((ny * q.shape[1] - deep, q.shape[2]), F32),
            jax.ShapeDtypeStruct((deep, q.shape[2]), F32),
            jax.ShapeDtypeStruct(py.shape, F32),
        ),
        in_specs=[VMEM] * 5,
        out_specs=(ANY, VMEM, VMEM, VMEM),
        scratch_shapes=scratch,
        compiler_params=pltpu.CompilerParams(collective_id=1, has_side_effects=True),
    )(w, gt, mask, q, py)


def flow_kernel(
    nx, ny, per_c, field, gauss, gauss_up, select, masks, east, north, up,
    r_ref, fx_out, fz_out, fy_out,
    g_ref, gu_ref, sel_ref, mask_ref, east_ref, north_ref, up_ref, fx_ref, fz_ref, fy_ref,
    n_buf, t_buf, f_buf, x_buf, y_buf, w_land, wf, w_own, w_in, u_buf, wt,
    q_buf, q_in, q_all, p_buf, y_in, z_in, z_own,
    s1, r1, l1, s2, r2, ws, wr, us, ur, ul, fs, os, ds, qs, qr, ys, yr, zs, zr, gs, gr,
):
    gx, gy = lax.axis_index("gx"), lax.axis_index("gy")
    spot, core = gy // 2, gy % 2
    last = ny // 2 - 1
    middle = jnp.logical_and(spot > 0, spot < last)
    left_half = spot * 2 < last
    end = jnp.where(left_half, 0, last)
    near = jnp.where(left_half, 1, last - 1)
    spots = (end, last - spot, last - end, spot)
    goals = (gy, 2 * spot + 1 - core, 2 * end, 2 * end + 1)

    span, rows, deep = f_buf.shape
    steps, share = x_buf.shape[:2]
    _, _, _, groups, tall, lanes = u_buf.shape
    a_in = mask_ref.shape[0]
    a_rows = groups * a_in
    width = up_ref.shape[1]
    x_rows, z_rows = rows // ny, deep // ny

    batch = n_buf.shape[2]
    loads = [
        pltpu.make_async_copy(field.at[:, c * batch : (c + 1) * batch, :], n_buf.at[c], fs.at[c])
        for c in range(span // batch)
    ]
    for copy in loads:
        copy.start()
    small_loads = [
        pltpu.make_async_copy(src, dst, os.at[k])
        for k, (src, dst) in enumerate(
            (
                (east, east_ref), (north, north_ref), (up, up_ref), (gauss, g_ref),
                (gauss_up, gu_ref), (select, sel_ref), (masks, mask_ref),
            )
        )
    ]
    for copy in small_loads:
        copy.start()
    barrier = pltpu.get_barrier_semaphore()
    for d in range(1, ny):
        pl.semaphore_signal(barrier, inc=1, device_id=(gx, lax.rem(gy + d, ny)), device_id_type=MESH)
    for d in range(1, nx):
        pl.semaphore_signal(barrier, inc=1, device_id=(lax.rem(gx + d, nx), gy), device_id_type=MESH)
    pl.semaphore_wait(barrier, nx + ny - 2)

    def send(src, dst, ssem, rsem, where):
        return pltpu.make_async_remote_copy(
            src_ref=src, dst_ref=dst, send_sem=ssem, recv_sem=rsem, device_id=where, device_id_type=MESH
        )

    def first(m, d):
        to = lax.rem(gx + d, nx)
        src = f_buf.at[pl.ds(m * tall + to * share, share)]
        dst = x_buf.at[m, :, pl.ds(pl.multiple_of(gx * rows, rows), rows), :]
        if d == nx:
            return pltpu.make_async_copy(src, dst, l1.at[m])
        return send(src, dst, s1.at[m, d], r1.at[m, d], (to, gy))

    def second(m, d):
        to = lax.rem(gx + d, nx)
        return send(y_buf.at[m, d - 1], w_land.at[m, gx], s2.at[m, d], r2.at[m, d], (to, gy))

    def send_first(m):
        for d in range(1, nx + 1):
            first(m, d).start()

    def mix_first(m):
        first(m, nx).wait()
        for d in range(1, nx):
            first(m, d).wait_recv()
        block = jnp.concatenate([x_buf[m, j] for j in range(share)], axis=1)
        for d in range(1, nx + 1):
            to = lax.rem(gx + d, nx)
            got = jnp.dot(g_ref[to], block, preferred_element_type=F32).astype(BF)
            if d < nx:
                y_buf[m, d - 1] = got
                second(m, d).start()
            else:
                w_land[m, gx] = got

    def raw(src, slot, m, to_spot):
        return send(src, w_in.at[slot, m], ws.at[slot, m], wr.at[slot, m], (gx, 2 * to_spot + core))

    def place(m, origin):
        return r_ref.at[:, pl.ds(pl.multiple_of(origin * span + m * tall, tall), tall), :]

    def block(kind, slot, m):
        source = 2 * spots[slot] + core
        if kind == 0:
            return pltpu.make_async_copy(u_buf.at[kind, slot, m], place(m, source), ul.at[slot, m])
        return send(
            u_buf.at[kind, slot, m], place(m, source), us.at[kind, slot, m],
            ur.at[m, spots[slot], core], (gx, goals[kind]),
        )

    def arrived(m, at, side):
        send(
            u_buf.at[0, 0, m], place(m, 2 * at + side), us.at[1, 0, m], ur.at[m, at, side], (gx, goals[1])
        ).wait_recv()

    pieces, base = [], 0
    for tile in range(lanes // 128):
        low = min(tile * 128 // per_c, a_in - 1)
        high = min((tile * 128 + 127) // per_c, a_in - 1)
        pieces.append((tile, low, high, base))
        base += (high + 1 - low) * deep

    def weigh(kind):
        mine = gu_ref[pl.ds(pl.multiple_of(goals[kind] * per_c, per_c), per_c), :]
        spread = lax.dot_general(
            mine, sel_ref[...], (((0,), (0,)), ((), ())), preferred_element_type=F32
        )
        for tile, low, high, at in pieces:
            here = slice(tile * 128, tile * 128 + 128)
            for k in range(low, high + 1):
                wt[kind, at + (k - low) * deep : at + (k - low + 1) * deep] = (
                    spread[:, here] * mask_ref[k : k + 1, here]
                ).astype(BF)

    def mix(kind, slot, m, left):
        for tile, low, high, at in pieces:
            got = jnp.dot(
                left[:, low * deep : (high + 1) * deep],
                wt[kind, at : at + (high + 1 - low) * deep],
                preferred_element_type=F32,
            )
            u_buf[kind, slot, m, :, :, tile * 128 : tile * 128 + 128] = (
                got.reshape(groups, tall, 128).astype(BF)
            )
        block(kind, slot, m).start()

    def settle(m):
        for d in range(1, nx):
            second(m, d).wait_recv()
        for y in range(tall):
            at = (y % share) * deep
            wf[pl.ds(y, a_rows, stride=tall), :] = w_land[m, y // share, :, at : at + deep].astype(F32)
        for k in range(a_in):
            part = jnp.concatenate(
                [wf[(g * a_in + k) * tall : (g * a_in + k + 1) * tall, :] for g in range(groups)], axis=0
            )
            w_own[m, :, k * deep : (k + 1) * deep] = part.astype(BF)

    def sketch():
        step = 16 if span % 16 == 0 else span
        along_x = east_ref[...].astype(F32)[None]
        part_x = jnp.zeros((rows, width), F32)
        part_z = jnp.zeros((deep, width), F32)
        for c in range(0, span, step):
            cells = f_buf[c : c + step].reshape(step * rows, deep)
            along_y = north_ref[c : c + step].astype(F32)[:, None, :]
            weighted = jnp.dot(cells, up_ref[...], preferred_element_type=F32).reshape(step, rows, width)
            p_buf[c : c + step] = jnp.sum(weighted * along_x, axis=1)
            part_x = part_x + jnp.sum(weighted * along_y, axis=0)
            khatri = (along_x * along_y).astype(BF).reshape(step * rows, width)
            part_z = part_z + lax.dot_general(
                cells, khatri, (((0,), (0,)), ((), ())), preferred_element_type=F32
            )
        for k in range(ny):
            q_buf[k, :x_rows] = part_x[k * x_rows : (k + 1) * x_rows]
            q_buf[k, x_rows:] = part_z[k * z_rows : (k + 1) * z_rows]

    def small(d):
        to = lax.rem(gy + d, ny)
        return send(q_buf.at[to], q_in.at[d], qs.at[d], qr.at[d], (gx, to))

    def small_y(d):
        to = lax.rem(gx + d, nx)
        return send(p_buf, y_in.at[d], ys.at[d], yr.at[d], (to, gy))

    def small_z(d):
        to = lax.rem(gx + d, nx)
        return send(z_own, z_in.at[d], zs.at[d], zr.at[d], (to, gy))

    def gather(d):
        to = lax.rem(gy + d, ny)
        return send(q_all.at[gy], q_all.at[gy], gs.at[d], gr.at[d], (gx, to))

    def gathered(d):
        source = lax.rem(gy - d + ny, ny)
        return send(q_all.at[source], q_all.at[source], gs.at[d], gr.at[d], (gx, source))

    def turn(c):
        loads[c].wait()
        t_buf[...] = n_buf[c].astype(F32).reshape(rows * batch, deep)
        for y in range(batch):
            f_buf[c * batch + y] = t_buf[pl.ds(y, rows, stride=batch), :].astype(BF)

    turn(0)
    send_first(0)
    send_first(1)
    for c in range(1, span // batch):
        turn(c)
    for copy in small_loads:
        copy.wait()
    sketch()
    for d in range(1, ny):
        small(d).start()
    for d in range(1, nx):
        small_y(d).start()
    mix_first(0)
    send_first(2)
    for kind in range(4):
        weigh(kind)

    done_y = pltpu.make_async_copy(fy_ref, fy_out, ds.at[0])

    def stage(s, carry):
        @pl.when(s + 1 < steps)
        def _():
            mix_first(s + 1)

        @pl.when(s + 3 < steps)
        def _():
            send_first(s + 3)

        @pl.when(s < steps)
        def _():
            settle(s)

        @pl.when(jnp.logical_and(s < steps, middle))
        def _():
            raw(w_own.at[s], 1, s, last - spot).start()
            for kind in (2, 3):
                mix(kind, 3, s, w_own.at[s])

        @pl.when(jnp.logical_and(s < steps, jnp.logical_not(middle)))
        def _():
            raw(w_own.at[s], 0, s, near).start()

        @pl.when(s < steps)
        def _():
            for kind in (1, 0):
                mix(kind, 3, s, w_own.at[s])

        @pl.when(jnp.logical_and(jnp.logical_and(s >= 1, s < steps + 1), middle))
        def _():
            m = s - 1
            raw(w_own.at[m], 0, m, near).wait_recv()
            raw(w_in.at[0, m], 2, m, last - spot).start()
            raw(w_own.at[m], 1, m, last - spot).wait_recv()
            for kind, slot in ((2, 1), (3, 1), (1, 1), (0, 1), (1, 0), (0, 0)):
                mix(kind, slot, m, w_in.at[slot, m])

        @pl.when(jnp.logical_and(s >= 2, middle))
        def _():
            m = s - 2
            raw(w_in.at[0, m], 2, m, last - spot).wait_recv()
            for kind in (2, 3, 1, 0):
                mix(kind, 2, m, w_in.at[2, m])

        @pl.when(s == 1)
        def _():
            for d in range(1, ny):
                small(d).wait()
            total = q_buf[gy]
            for d in range(1, ny):
                total = total + q_in[d]
            q_all[gy] = total
            z_own[...] = total[x_rows:]
            for d in range(1, nx):
                small_z(d).start()

        @pl.when(s == 3)
        def _():
            for d in range(1, nx):
                small_y(d).wait()
                small_z(d).wait()
            y_in[0] = p_buf[...]
            z_in[0] = z_own[...]
            y_total = jnp.zeros(p_buf.shape, F32)
            z_total = jnp.zeros(z_own.shape, F32)
            for g in range(nx):
                y_total = y_total + y_in[lax.rem(gx - g + nx, nx)]
                z_total = z_total + z_in[lax.rem(gx - g + nx, nx)]
            fy_ref[...] = y_total
            done_y.start()
            q_all[gy, x_rows:] = z_total
            for d in range(1, ny):
                gather(d).start()

        return carry

    lax.fori_loop(0, steps + 2, stage, 0)

    for d in range(1, ny):
        gather(d).wait_send()
        gathered(d).wait_recv()
    for k in range(ny):
        fx_ref[k * x_rows : (k + 1) * x_rows] = q_all[k, :x_rows]
        fz_ref[k * z_rows : (k + 1) * z_rows] = q_all[k, x_rows:]
    done_x = pltpu.make_async_copy(fx_ref, fx_out, ds.at[1])
    done_z = pltpu.make_async_copy(fz_ref, fz_out, ds.at[2])
    done_x.start()
    done_z.start()

    def close(m, carry):
        for d in range(1, nx):
            first(m, d).wait_send()
            second(m, d).wait_send()
        block(0, 3, m).wait()
        block(1, 3, m).wait_send()
        arrived(m, spot, 1 - core)

        @pl.when(middle)
        def _():
            raw(w_own.at[m], 1, m, last - spot).wait_send()
            raw(w_in.at[0, m], 2, m, last - spot).wait_send()
            block(2, 3, m).wait_send()
            block(3, 3, m).wait_send()
            for slot in range(3):
                block(0, slot, m).wait()
                block(1, slot, m).wait_send()
                if slot:
                    block(2, slot, m).wait_send()
                    block(3, slot, m).wait_send()
                arrived(m, spots[slot], 1 - core)

        @pl.when(jnp.logical_not(middle))
        def _():
            raw(w_own.at[m], 0, m, near).wait_send()
            for d in range(1, ny // 2):
                for side in range(2):
                    arrived(m, lax.rem(spot + d, ny // 2), side)

        return carry

    lax.fori_loop(0, steps, close, 0)
    for copy in (done_x, done_y, done_z):
        copy.wait()


def flow(field, gauss_east, gauss_up, east, north, up, nx, ny, a_in, lanes):
    rows, span, deep = field.shape
    a_rows = gauss_east.shape[0] // nx
    per_c = gauss_up.shape[0] // ny
    groups = a_rows // a_in
    tall = 8
    steps, share = span // tall, tall // nx
    width = up.shape[1]
    x_rows, z_rows = rows // ny, deep // ny
    lane = np.arange(lanes)
    used = lane < a_in * per_c
    sel = np.logical_and(lane[None] % per_c == np.arange(per_c)[:, None], used[None]).astype(np.float32)
    mask = (lane[None] // per_c == np.arange(a_in)[:, None]).astype(np.float32)
    total_k = sum(
        min((t * 128 + 127) // per_c, a_in - 1) + 1 - min(t * 128 // per_c, a_in - 1)
        for t in range(lanes // 128)
    ) * deep
    dma = lambda *shape: pltpu.SemaphoreType.DMA(shape)
    vm = pltpu.VMEM
    q_shape = (ny, x_rows + z_rows, width)
    batch = 16 if span % 16 == 0 else tall
    scratch = [
        vm((nx, a_rows, gauss_east.shape[1]), BF), vm(gauss_up.shape, BF), vm(sel.shape, BF),
        vm(mask.shape, F32), vm(east.shape, BF), vm(north.shape, BF), vm(up.shape, BF),
        vm((rows, width), F32), vm((deep, width), F32), vm((span, width), F32),
        vm((span // batch, rows, batch, deep), BF),
        vm((rows * batch, deep), F32),
        vm((span, rows, deep), BF),
        vm((steps, share, nx * rows, deep), BF),
        vm((steps, nx - 1, a_rows, share * deep), BF),
        vm((steps, nx, a_rows, share * deep), BF),
        vm((a_rows * tall, deep), F32),
        vm((steps, groups * tall, a_in * deep), BF),
        vm((3, steps, groups * tall, a_in * deep), BF),
        vm((4, 4, steps, groups, tall, lanes), BF),
        vm((4, total_k, 128), BF),
        vm(q_shape, F32), vm(q_shape, F32), vm(q_shape, F32),
        vm((span, width), F32), vm((nx, span, width), F32),
        vm((nx, z_rows, width), F32), vm((z_rows, width), F32),
        dma(steps, nx), dma(steps, nx), dma(steps), dma(steps, nx), dma(steps, nx),
        dma(3, steps), dma(3, steps), dma(4, 4, steps), dma(steps, ny // 2, 2), dma(4, steps),
        dma(span // batch), dma(7), dma(3),
        dma(ny), dma(ny), dma(nx), dma(nx), dma(nx), dma(nx), dma(ny), dma(ny),
    ]
    return pl.pallas_call(
        functools.partial(flow_kernel, nx, ny, per_c),
        out_shape=(
            pltpu.VMEM((groups, ny * span, lanes), BF),
            jax.ShapeDtypeStruct((rows, width), F32),
            jax.ShapeDtypeStruct((deep, width), F32),
            jax.ShapeDtypeStruct((span, width), F32),
        ),
        in_specs=[ANY] * 8,
        out_specs=(VMEM, ANY, ANY, ANY),
        scratch_shapes=scratch,
        compiler_params=pltpu.CompilerParams(collective_id=2, has_side_effects=True),
    )(
        field, gauss_east.reshape(nx, a_rows, -1), gauss_up,
        jnp.asarray(sel, BF), jnp.asarray(mask, F32), east, north, up,
    )


def mix_y_kernel(
    take, r_ref, g_ref, fx_ref, fy_ref, fz_ref, o_ref, fx_out, fy_out, fz_out,
    g_buf, o_buf, fx_buf, fy_buf, fz_buf, gs, os, fs, ts,
):
    groups = o_buf.shape[0]
    load = pltpu.make_async_copy(g_ref, g_buf, gs.at[0])
    load.start()
    trios = ((fx_ref, fx_buf, fx_out), (fy_ref, fy_buf, fy_out), (fz_ref, fz_buf, fz_out))
    ins = [pltpu.make_async_copy(src, mid, fs.at[k]) for k, (src, mid, _) in enumerate(trios)]
    stores = [pltpu.make_async_copy(mid, dst, ts.at[k]) for k, (_, mid, dst) in enumerate(trios)]
    for copy in ins:
        copy.start()
    load.wait()
    for c in range(0, groups, take):
        for k in range(c, c + take):
            o_buf[k] = lax.dot_general(
                r_ref[k], g_buf[...], (((0,), (1,)), ((), ())), preferred_element_type=F32
            )
        store = pltpu.make_async_copy(
            o_buf.at[pl.ds(c, take)], o_ref.at[pl.ds(c, take)], os.at[c // take]
        )
        store.start()
        stores.append(store)
        if c == 0:
            for k in range(3):
                ins[k].wait()
                stores[k].start()
    for copy in stores:
        copy.wait()


def mix_y(r, g, fx, fy, fz):
    groups, deep, lanes = r.shape
    out = g.shape[0]
    take = 1 if groups % 1 == 0 else 1
    dma = lambda *shape: pltpu.SemaphoreType.DMA(shape)
    vm = pltpu.VMEM
    like = lambda x: jax.ShapeDtypeStruct(x.shape, x.dtype)
    return pl.pallas_call(
        functools.partial(mix_y_kernel, take),
        out_shape=(jax.ShapeDtypeStruct((groups, lanes, out), F32), like(fx), like(fy), like(fz)),
        in_specs=[VMEM, ANY, ANY, ANY, ANY],
        out_specs=(ANY, ANY, ANY, ANY),
        scratch_shapes=[
            vm(g.shape, BF), vm((groups, lanes, out), F32), vm(fx.shape, F32), vm(fy.shape, F32),
            vm(fz.shape, F32), dma(1), dma(groups // take), dma(3), dma(3),
        ],
    )(r, g, fx, fy, fz)


def per_device(
    nx, ny,
    thermal_field,
    probe_range_east,
    probe_range_north,
    probe_range_upward,
    gauss_kernel_east,
    gauss_kernel_north,
    gauss_kernel_upward,
):
    rows, span, deep = thermal_field.shape
    a_rows = gauss_kernel_east.shape[0] // nx
    per_c = gauss_kernel_upward.shape[0] // ny
    a_in = 8 if a_rows % 8 == 0 and 8 * per_c % 128 == 0 else a_rows
    groups = a_rows // a_in
    used = a_in * per_c
    lanes = -(-used // 128) * 128

    if ny == 8 and 8 % nx == 0 and span % 8 == 0 and span // 8 > 2 and a_in % 8 == 0 and per_c % 16 == 0:
        r, factor_x, factor_z, factor_y = flow(
            thermal_field, gauss_kernel_east, gauss_kernel_upward,
            probe_range_east, probe_range_north, probe_range_upward, nx, ny, a_in, lanes,
        )
        r = pltpu.with_memory_space_constraint(r, pltpu.VMEM)
    else:
        w, q, part_y = mix_x(
            thermal_field.reshape(rows, span * deep),
            gauss_kernel_east.reshape(nx, a_rows, -1),
            nx,
            a_rows,
            thermal_field,
            probe_range_east,
            probe_range_north,
            probe_range_upward,
            ny,
        )
        w = w.reshape(groups, a_in, span, deep).transpose(0, 2, 1, 3).reshape(groups * span, a_in * deep)

        gt = gauss_kernel_upward.reshape(ny, per_c, deep).transpose(0, 2, 1)
        gt = jnp.pad(jnp.tile(gt, (1, 1, a_in)), ((0, 0), (0, 0), (0, lanes - used)))
        mask = (
            lax.broadcasted_iota(jnp.int32, (a_in, lanes), 1) // per_c
            == lax.broadcasted_iota(jnp.int32, (a_in, lanes), 0)
        ).astype(BF)
        r, factor_x, factor_z, factor_y = exchange(w, gt, mask, q, part_y, nx, ny, groups, span, per_c)

    core, factor_x, factor_y, factor_z = mix_y(r, gauss_kernel_north, factor_x, factor_y, factor_z)
    core = core[:, :used].reshape(a_rows, per_c, -1).transpose(0, 2, 1)
    return (factor_x, factor_y, factor_z, core)


def solution(mesh):
    in_specs = (P("gx", "gy", None), P("gx", None), P("gy", None), P(), P(), P(), P())
    out_specs = (P("gx", None), P("gy", None), P(), P("gx", None, "gy"))
    body = functools.partial(per_device, mesh.shape["gx"], mesh.shape["gy"])
    return jax.shard_map(
        body, mesh=mesh, in_specs=in_specs, out_specs=out_specs, check_vma=False
    )
```

```python
import functools

import jax
import jax.numpy as jnp
import numpy as np
from jax import lax
from jax.experimental import pallas as pl
from jax.experimental.pallas import tpu as pltpu
from jax.sharding import PartitionSpec as P

MESH = pl.DeviceIdType.MESH
VMEM = pl.BlockSpec(memory_space=pltpu.VMEM)
ANY = pl.BlockSpec(memory_space=pl.ANY)
BF = jnp.bfloat16
F32 = jnp.float32


def remote(src, dst, send, recv, where):
    copy = pltpu.make_async_remote_copy(
        src_ref=src, dst_ref=dst, send_sem=send, recv_sem=recv, device_id=where, device_id_type=MESH
    )
    copy.start()
    return copy


def sketch_parts(f_ref, east_ref, north_ref, up_ref, q_ref, py_ref, px_buf):
    rows, span, deep = f_ref.shape
    width = up_ref.shape[1]
    step = 16 if rows % 16 == 0 else rows
    along_y = north_ref[...].astype(F32)
    part_y = jnp.zeros((span, width), F32)
    part_z = jnp.zeros((deep, width), F32)
    for c in range(0, rows, step):
        cells = f_ref[c : c + step].reshape(step * span, deep)
        along_x = east_ref[c : c + step].astype(F32)
        weighted = jnp.dot(cells, up_ref[...], preferred_element_type=F32).reshape(step, span, width)
        px_buf[c : c + step] = jnp.sum(weighted * along_y[None, :, :], axis=1)
        part_y = part_y + jnp.sum(weighted * along_x[:, None, :], axis=0)
        khatri = (along_x[:, None, :] * along_y[None, :, :]).astype(BF).reshape(step * span, width)
        part_z = part_z + lax.dot_general(
            cells, khatri, (((0,), (0,)), ((), ())), preferred_element_type=F32
        )
    py_ref[...] = part_y
    ny = q_ref.shape[0]
    x_rows, z_rows = rows // ny, deep // ny
    for k in range(ny):
        q_ref[k, :x_rows] = px_buf[k * x_rows : (k + 1) * x_rows]
        q_ref[k, x_rows:] = part_z[k * z_rows : (k + 1) * z_rows]


def mix_x_kernel(
    n, chunks, t_ref, g_ref, f_ref, east_ref, north_ref, up_ref, w_ref, q_ref, py_ref,
    x_buf, y_buf, px_buf, s1, r1, s2, r2, ls,
):
    gx, gy = lax.axis_index("gx"), lax.axis_index("gy")
    rows = t_ref.shape[0]
    a_rows = y_buf.shape[2]
    wide = t_ref.shape[1] // n
    part = wide // chunks
    barrier = pltpu.get_barrier_semaphore()
    for d in range(1, n):
        pl.semaphore_signal(barrier, inc=1, device_id=(lax.rem(gx + d, n), gy), device_id_type=MESH)
    pl.semaphore_wait(barrier, n - 1)

    first, second, local = [], [], []
    for m in range(chunks):
        for d in range(1, n):
            to = lax.rem(gx + d, n)
            lanes = pl.ds(pl.multiple_of(to * wide + m * part, 128), part)
            first.append(
                remote(t_ref.at[:, lanes], x_buf.at[m, gx], s1.at[m, d], r1.at[m, d], (to, gy))
            )
        lanes = pl.ds(pl.multiple_of(gx * wide + m * part, 128), part)
        own = pltpu.make_async_copy(t_ref.at[:, lanes], x_buf.at[m, gx], ls.at[m, 0])
        own.start()
        local.append(own)
    sketch_parts(f_ref, east_ref, north_ref, up_ref, q_ref, py_ref, px_buf)
    for m in range(chunks):
        local[m].wait()
        for d in range(1, n):
            first[m * (n - 1) + d - 1].wait()
        block = x_buf[m].reshape(n * rows, part)
        lanes = pl.ds(pl.multiple_of(gx * wide + m * part, 128), part)
        for d in range(1, n + 1):
            to = lax.rem(gx + d, n)
            y_buf[m, d - 1] = jnp.dot(g_ref[to], block, preferred_element_type=F32).astype(BF)
            if d < n:
                second.append(
                    remote(
                        y_buf.at[m, d - 1], w_ref.at[:, lanes], s2.at[m, d], r2.at[m, d], (to, gy)
                    )
                )
            else:
                own = pltpu.make_async_copy(y_buf.at[m, d - 1], w_ref.at[:, lanes], ls.at[m, 1])
                own.start()
                second.append(own)
    for copy in second:
        copy.wait()


def mix_x(field, gauss, n, a_rows, cells, east, north, up, ny):
    rows, lanes = field.shape
    wide = lanes // n
    chunks = 3 if wide % 384 == 0 else 1
    dma = lambda *shape: pltpu.SemaphoreType.DMA(shape)
    return pl.pallas_call(
        functools.partial(mix_x_kernel, n, chunks),
        out_shape=(
            jax.ShapeDtypeStruct((a_rows, lanes), BF),
            jax.ShapeDtypeStruct((ny, (cells.shape[0] + cells.shape[2]) // ny, up.shape[1]), F32),
            jax.ShapeDtypeStruct(north.shape, F32),
        ),
        in_specs=[VMEM] * 6,
        out_specs=(VMEM, VMEM, VMEM),
        scratch_shapes=[
            pltpu.VMEM((chunks, n, rows, wide // chunks), BF),
            pltpu.VMEM((chunks, n, a_rows, wide // chunks), BF),
            pltpu.VMEM(east.shape, F32),
            dma(chunks, n), dma(chunks, n), dma(chunks, n), dma(chunks, n), dma(chunks, 2),
        ],
        compiler_params=pltpu.CompilerParams(collective_id=0, has_side_effects=True),
    )(field, gauss, cells, east, north, up)


def exchange_kernel(
    nx, ny, batches, per_c, w_ref, gt_ref, mask_ref, q_ref, py_ref,
    r_ref, fx_ref, fz_ref, pyo_ref,
    u_buf, q_in, q_all, y_in, z_in, z_own,
    us, ur, ul, qs, qr, ys, yr, zs, zr, gs, gr,
):
    gx, gy = lax.axis_index("gx"), lax.axis_index("gy")
    span = u_buf.shape[3]
    per = u_buf.shape[2]
    lanes = u_buf.shape[4]
    a_in = mask_ref.shape[0]
    deep = gt_ref.shape[1]
    x_rows = q_ref.shape[1] - z_in.shape[1]
    barrier = pltpu.get_barrier_semaphore()
    for d in range(1, ny):
        pl.semaphore_signal(barrier, inc=1, device_id=(gx, lax.rem(gy + d, ny)), device_id_type=MESH)
    for d in range(1, nx):
        pl.semaphore_signal(barrier, inc=1, device_id=(lax.rem(gx + d, nx), gy), device_id_type=MESH)
    pl.semaphore_wait(barrier, nx + ny - 2)

    small, ysmall, big = [], [], []
    for d in range(1, ny):
        to = lax.rem(gy + d, ny)
        small.append(remote(q_ref.at[to], q_in.at[d], qs.at[d], qr.at[d], (gx, to)))
    for d in range(1, nx):
        to = lax.rem(gx + d, nx)
        ysmall.append(remote(py_ref, y_in.at[d], ys.at[d], yr.at[d], (to, gy)))

    rows_b = per * span
    for b in range(batches):
        for d in range(1, ny + 1):
            to = lax.rem(gy + d, ny)
            for tile in range(lanes // 128):
                low = min(tile * 128 // per_c, a_in - 1)
                high = min((tile * 128 + 127) // per_c, a_in - 1)
                here = slice(tile * 128, tile * 128 + 128)
                weights = jnp.concatenate(
                    [gt_ref[to, :, here] * mask_ref[k : k + 1, here] for k in range(low, high + 1)], axis=0
                )
                left = w_ref[b * rows_b : (b + 1) * rows_b, low * deep : (high + 1) * deep]
                got = jnp.dot(left, weights, preferred_element_type=F32).astype(BF)
                u_buf[b, d - 1, :, :, here] = got.reshape(per, span, 128)
            target = r_ref.at[pl.ds(b * per, per), pl.ds(pl.multiple_of(gy * span, span), span), :]
            if d < ny:
                big.append(remote(u_buf.at[b, d - 1], target, us.at[b, d], ur.at[b, d], (gx, to)))
            else:
                own = pltpu.make_async_copy(u_buf.at[b, d - 1], target, ul.at[b])
                own.start()
                big.append(own)
        if b == 0:
            for copy in small:
                copy.wait()
            total = q_ref[gy]
            for d in range(1, ny):
                total = total + q_in[d]
            z_own[...] = total[x_rows:]
            zsmall = []
            for d in range(1, nx):
                to = lax.rem(gx + d, nx)
                zsmall.append(remote(z_own, z_in.at[d], zs.at[d], zr.at[d], (to, gy)))
            for copy in ysmall:
                copy.wait()
            y_in[0] = py_ref[...]
            y_total = jnp.zeros(py_ref.shape, F32)
            for g in range(nx):
                y_total = y_total + y_in[lax.rem(gx - g + nx, nx)]
            pyo_ref[...] = y_total
    for copy in zsmall:
        copy.wait()
    z_in[0] = z_own[...]
    z_total = jnp.zeros(z_own.shape, F32)
    for g in range(nx):
        z_total = z_total + z_in[lax.rem(gx - g + nx, nx)]
    q_all[gy, :x_rows] = total[:x_rows]
    q_all[gy, x_rows:] = z_total
    gathers = []
    for d in range(1, ny):
        to = lax.rem(gy + d, ny)
        gathers.append(remote(q_all.at[gy], q_all.at[gy], gs.at[d], gr.at[d], (gx, to)))
    for copy in gathers:
        copy.wait()
    z_rows = z_own.shape[0]
    for k in range(ny):
        fx_ref[k * x_rows : (k + 1) * x_rows] = q_all[k, :x_rows]
        fz_ref[k * z_rows : (k + 1) * z_rows] = q_all[k, x_rows:]
    for copy in big:
        copy.wait()


def line_kernel(
    nx, ny, batches, per_c, w_ref, gt_ref, mask_ref, q_ref, py_ref,
    r_ref, fx_ref, fz_ref, pyo_ref,
    w_in, u_buf, wt, q_in, q_all, y_in, z_in, z_own,
    ws, wr, us, ur, ul, qs, qr, ys, yr, zs, zr, gs, gr,
):
    gx, gy = lax.axis_index("gx"), lax.axis_index("gy")
    spot, core = gy // 2, gy % 2
    last = ny // 2 - 1
    middle = jnp.logical_and(spot > 0, spot < last)
    left_half = spot * 2 < last
    end = jnp.where(left_half, 0, last)
    near = jnp.where(left_half, 1, last - 1)
    _, _, _, per, span, lanes = u_buf.shape
    a_in = mask_ref.shape[0]
    deep = gt_ref.shape[1]
    x_rows = q_ref.shape[1] - z_in.shape[1]
    rows_b = per * span
    spots = (end, last - spot, last - end, spot)
    goals = (gy, 2 * spot + 1 - core, 2 * end, 2 * end + 1)
    barrier = pltpu.get_barrier_semaphore()
    for d in range(1, ny):
        pl.semaphore_signal(barrier, inc=1, device_id=(gx, lax.rem(gy + d, ny)), device_id_type=MESH)
    for d in range(1, nx):
        pl.semaphore_signal(barrier, inc=1, device_id=(lax.rem(gx + d, nx), gy), device_id_type=MESH)
    pl.semaphore_wait(barrier, nx + ny - 2)

    small, ysmall = [], []
    for d in range(1, ny):
        to = lax.rem(gy + d, ny)
        small.append(remote(q_ref.at[to], q_in.at[d], qs.at[d], qr.at[d], (gx, to)))
    for d in range(1, nx):
        to = lax.rem(gx + d, nx)
        ysmall.append(remote(py_ref, y_in.at[d], ys.at[d], yr.at[d], (to, gy)))

    def raw(src, slot, b, to_spot):
        return pltpu.make_async_remote_copy(
            src_ref=src, dst_ref=w_in.at[slot, b], send_sem=ws.at[slot, b], recv_sem=wr.at[slot, b],
            device_id=(gx, 2 * to_spot + core), device_id_type=MESH,
        )

    def rows_of(b):
        return w_ref.at[pl.ds(b * rows_b, rows_b), :]

    def place(b, origin):
        return r_ref.at[pl.ds(b * per, per), pl.ds(pl.multiple_of(origin * span, span), span), :]

    def block(kind, slot, b):
        source = 2 * spots[slot] + core
        if kind == 0:
            return pltpu.make_async_copy(u_buf.at[kind, slot, b], place(b, source), ul.at[slot, b])
        return pltpu.make_async_remote_copy(
            src_ref=u_buf.at[kind, slot, b], dst_ref=place(b, source),
            send_sem=us.at[kind, slot, b], recv_sem=ur.at[b, spots[slot], core],
            device_id=(gx, goals[kind]), device_id_type=MESH,
        )

    def arrived(b, at, side):
        pltpu.make_async_remote_copy(
            src_ref=u_buf.at[0, 0, b], dst_ref=place(b, 2 * at + side),
            send_sem=us.at[1, 0, b], recv_sem=ur.at[b, at, side],
            device_id=(gx, goals[1]), device_id_type=MESH,
        ).wait_recv()

    pieces, base = [], 0
    for tile in range(lanes // 128):
        low = min(tile * 128 // per_c, a_in - 1)
        high = min((tile * 128 + 127) // per_c, a_in - 1)
        pieces.append((tile, low, high, base))
        base += (high + 1 - low) * deep

    def weigh(kind):
        for tile, low, high, at in pieces:
            here = slice(tile * 128, tile * 128 + 128)
            for k in range(low, high + 1):
                wt[kind, at + (k - low) * deep : at + (k - low + 1) * deep] = (
                    gt_ref[goals[kind], :, here] * mask_ref[k : k + 1, here]
                )

    def mix(kind, slot, b, left):
        for tile, low, high, at in pieces:
            got = jnp.dot(
                left[:, low * deep : (high + 1) * deep],
                wt[kind, at : at + (high + 1 - low) * deep],
                preferred_element_type=F32,
            ).astype(BF)
            u_buf[kind, slot, b, :, :, tile * 128 : tile * 128 + 128] = got.reshape(per, span, 128)

    def own_blocks(kind):
        weigh(kind)
        for b in range(batches):
            mix(kind, 3, b, rows_of(b))
            block(kind, 3, b).start()

    @pl.when(middle)
    def _():
        for b in range(batches):
            raw(rows_of(b), 1, b, last - spot).start()
        for kind in (2, 3):
            own_blocks(kind)

    @pl.when(jnp.logical_not(middle))
    def _():
        for b in range(batches):
            raw(rows_of(b), 0, b, near).start()

    for kind in (1, 0):
        own_blocks(kind)

    for copy in small:
        copy.wait()
    total = q_ref[gy]
    for d in range(1, ny):
        total = total + q_in[d]
    z_own[...] = total[x_rows:]
    zsmall = []
    for d in range(1, nx):
        to = lax.rem(gx + d, nx)
        zsmall.append(remote(z_own, z_in.at[d], zs.at[d], zr.at[d], (to, gy)))
    for copy in ysmall:
        copy.wait()
    y_in[0] = py_ref[...]
    y_total = jnp.zeros(py_ref.shape, F32)
    for g in range(nx):
        y_total = y_total + y_in[lax.rem(gx - g + nx, nx)]
    pyo_ref[...] = y_total
    for copy in zsmall:
        copy.wait()
    z_in[0] = z_own[...]
    z_total = jnp.zeros(z_own.shape, F32)
    for g in range(nx):
        z_total = z_total + z_in[lax.rem(gx - g + nx, nx)]
    q_all[gy, :x_rows] = total[:x_rows]
    q_all[gy, x_rows:] = z_total
    gathers = []
    for d in range(1, ny):
        to = lax.rem(gy + d, ny)
        gathers.append(remote(q_all.at[gy], q_all.at[gy], gs.at[d], gr.at[d], (gx, to)))

    @pl.when(middle)
    def _():
        for b in range(batches):
            raw(rows_of(b), 0, b, near).wait_recv()
            raw(w_in.at[0, b], 2, b, last - spot).start()
            raw(rows_of(b), 1, b, last - spot).wait_recv()
            for kind, slot in ((2, 1), (3, 1), (1, 1), (1, 0), (0, 1), (0, 0)):
                mix(kind, slot, b, w_in.at[slot, b])
                block(kind, slot, b).start()
        for b in range(batches):
            raw(w_in.at[0, b], 2, b, last - spot).wait_recv()
            for kind in (2, 3, 1, 0):
                mix(kind, 2, b, w_in.at[2, b])
                block(kind, 2, b).start()
        for b in range(batches):
            raw(rows_of(b), 1, b, last - spot).wait_send()
            raw(w_in.at[0, b], 2, b, last - spot).wait_send()
            for slot in range(4):
                block(0, slot, b).wait()
                block(1, slot, b).wait_send()
                if slot:
                    block(2, slot, b).wait_send()
                    block(3, slot, b).wait_send()
                arrived(b, spots[slot], 1 - core)

    @pl.when(jnp.logical_not(middle))
    def _():
        for b in range(batches):
            raw(rows_of(b), 0, b, near).wait_send()
            block(0, 3, b).wait()
            block(1, 3, b).wait_send()
            arrived(b, spot, 1 - core)
            for d in range(1, ny // 2):
                for side in range(2):
                    arrived(b, lax.rem(spot + d, ny // 2), side)

    for copy in gathers:
        copy.wait()
    z_rows = z_own.shape[0]
    for k in range(ny):
        fx_ref[k * x_rows : (k + 1) * x_rows] = q_all[k, :x_rows]
        fz_ref[k * z_rows : (k + 1) * z_rows] = q_all[k, x_rows:]


def exchange(w, gt, mask, q, py, nx, ny, groups, span, per_c):
    lanes = gt.shape[2]
    deep = gt.shape[1]
    z_rows = deep // ny
    dma = lambda *shape: pltpu.SemaphoreType.DMA(shape)
    vm = pltpu.VMEM
    sums = [
        vm(q.shape, F32), vm(q.shape, F32), vm((nx,) + py.shape, F32),
        vm((nx, z_rows, q.shape[2]), F32), vm((z_rows, q.shape[2]), F32),
    ]
    sum_sems = [dma(ny), dma(ny), dma(nx), dma(nx), dma(nx), dma(nx), dma(ny), dma(ny)]
    if ny == 8 and groups % 4 == 0:
        batches = 4
        per = groups // batches
        total_k = sum(
            min((t * 128 + 127) // per_c, mask.shape[0] - 1) + 1 - t * 128 // per_c
            for t in range(lanes // 128)
        ) * deep
        body = functools.partial(line_kernel, nx, ny, batches, per_c)
        scratch = [
            vm((3, batches, per * span, w.shape[1]), BF),
            vm((4, 4, batches, per, span, lanes), BF),
            vm((4, total_k, 128), BF),
        ] + sums + [
            dma(3, batches), dma(3, batches), dma(4, 4, batches), dma(batches, ny // 2, 2),
            dma(4, batches),
        ] + sum_sems
    else:
        batches = 3 if groups % 3 == 0 else 1
        per = groups // batches
        body = functools.partial(exchange_kernel, nx, ny, batches, per_c)
        scratch = [vm((batches, ny, per, span, lanes), BF)] + sums + [
            dma(batches, ny), dma(batches, ny), dma(batches)
        ] + sum_sems
    return pl.pallas_call(
        body,
        out_shape=(
            jax.ShapeDtypeStruct((groups, ny * span, lanes), BF),
            jax.ShapeDtypeStruct((ny * q.shape[1] - deep, q.shape[2]), F32),
            jax.ShapeDtypeStruct((deep, q.shape[2]), F32),
            jax.ShapeDtypeStruct(py.shape, F32),
        ),
        in_specs=[VMEM] * 5,
        out_specs=(ANY, VMEM, VMEM, VMEM),
        scratch_shapes=scratch,
        compiler_params=pltpu.CompilerParams(collective_id=1, has_side_effects=True),
    )(w, gt, mask, q, py)


def flow_kernel(
    nx, ny, per_c, field, gauss, gauss_up, select, masks, east, north, up,
    r_ref, fx_out, fz_out, fy_out,
    g_ref, gu_ref, sel_ref, mask_ref, east_ref, north_ref, up_ref, fx_ref, fz_ref, fy_ref,
    n_buf, t_buf, f_buf, x_buf, y_buf, w_land, wf, w_own, w_in, u_buf, wt,
    q_buf, q_in, q_all, p_buf, y_in, z_in, z_own,
    s1, r1, l1, s2, r2, ps, pr, ws, wr, us, ur, ul, fs, os, ds, qs, qr, ys, yr, zs, zr, gs, gr,
):
    gx, gy = lax.axis_index("gx"), lax.axis_index("gy")
    spot, core = gy // 2, gy % 2
    last = ny // 2 - 1
    middle = jnp.logical_and(spot > 0, spot < last)
    left_half = spot * 2 < last
    end = jnp.where(left_half, 0, last)
    near = jnp.where(left_half, 1, last - 1)
    spots = (end, last - spot, last - end, spot)
    goals = (gy, 2 * spot + 1 - core, 2 * end, 2 * end + 1)

    _, rows, deep = f_buf.shape
    share = x_buf.shape[1]
    span = north_ref.shape[0]
    _, _, steps, groups, tall, lanes = u_buf.shape
    ahead = x_buf.shape[0] - steps
    late = steps - ahead
    a_in = mask_ref.shape[0]
    a_rows = groups * a_in
    width = up_ref.shape[1]
    x_rows, z_rows = rows // ny, deep // ny

    batch = n_buf.shape[2]
    loads = [
        pltpu.make_async_copy(field.at[:, c * batch : (c + 1) * batch, :], n_buf.at[c], fs.at[c])
        for c in range(span // batch)
    ]
    for copy in loads:
        copy.start()
    small_loads = [
        pltpu.make_async_copy(src, dst, os.at[k])
        for k, (src, dst) in enumerate(
            (
                (east, east_ref), (north, north_ref), (up, up_ref), (gauss, g_ref),
                (gauss_up, gu_ref), (select, sel_ref), (masks, mask_ref),
            )
        )
    ]
    for copy in small_loads:
        copy.start()
    barrier = pltpu.get_barrier_semaphore()
    for d in range(1, ny):
        pl.semaphore_signal(barrier, inc=1, device_id=(gx, lax.rem(gy + d, ny)), device_id_type=MESH)
    for d in range(1, nx):
        pl.semaphore_signal(barrier, inc=1, device_id=(lax.rem(gx + d, nx), gy), device_id_type=MESH)
    pl.semaphore_wait(barrier, nx + ny - 2)

    def send(src, dst, ssem, rsem, where):
        return pltpu.make_async_remote_copy(
            src_ref=src, dst_ref=dst, send_sem=ssem, recv_sem=rsem, device_id=where, device_id_type=MESH
        )

    def first(m, d):
        to = lax.rem(gx + d, nx)
        src = f_buf.at[pl.ds(m * tall + to * share, share)]
        dst = x_buf.at[m, :, pl.ds(pl.multiple_of(gx * rows, rows), rows), :]
        if d == nx:
            return pltpu.make_async_copy(src, dst, l1.at[m])
        return send(src, dst, s1.at[m, d], r1.at[m, d], (to, gy))

    def second(m, d):
        to = lax.rem(gx + d, nx)
        return send(y_buf.at[m, d - 1], w_land.at[m, gx], s2.at[m, d], r2.at[m, d], (to, gy))

    def early(j, way):
        to = jnp.where(way == 0, end, last - spot)
        return send(
            f_buf.at[pl.ds((late + j) * tall, tall)], f_buf.at[pl.ds(span + j * tall, tall)],
            ps.at[way, j], pr.at[j], (gx, 2 * to + core),
        )

    def send_first(m):
        for d in range(1, nx + 1):
            first(m, d).start()

    def mix_first(m):
        first(m, nx).wait()
        for d in range(1, nx):
            first(m, d).wait_recv()
        block = jnp.concatenate([x_buf[m, j] for j in range(share)], axis=1)
        for d in range(1, nx + 1):
            to = lax.rem(gx + d, nx)
            got = jnp.dot(g_ref[to], block, preferred_element_type=F32).astype(BF)
            if d < nx:
                y_buf[m, d - 1] = got
                second(m, d).start()
            else:
                w_land[m, gx] = got

    def raw(src, slot, m, to_spot):
        return send(src, w_in.at[slot, m], ws.at[slot, m], wr.at[slot, m], (gx, 2 * to_spot + core))

    def place(m, origin):
        return r_ref.at[:, pl.ds(pl.multiple_of(origin * span + m * tall, tall), tall), :]

    def block(kind, slot, m, chip=None):
        chip = spots[slot] if chip is None else chip
        source = 2 * chip + core
        if kind == 0:
            return pltpu.make_async_copy(u_buf.at[kind, slot, m], place(m, source), ul.at[slot, m])
        return send(
            u_buf.at[kind, slot, m], place(m, source), us.at[kind, slot, m],
            ur.at[m, chip, core], (gx, goals[kind]),
        )

    def arrived(m, at, side):
        send(
            u_buf.at[0, 0, m], place(m, 2 * at + side), us.at[1, 0, m], ur.at[m, at, side], (gx, goals[1])
        ).wait_recv()

    pieces, base = [], 0
    for tile in range(lanes // 128):
        low = min(tile * 128 // per_c, a_in - 1)
        high = min((tile * 128 + 127) // per_c, a_in - 1)
        pieces.append((tile, low, high, base))
        base += (high + 1 - low) * deep

    def weigh(kind):
        mine = gu_ref[pl.ds(pl.multiple_of(goals[kind] * per_c, per_c), per_c), :]
        spread = lax.dot_general(
            mine, sel_ref[...], (((0,), (0,)), ((), ())), preferred_element_type=F32
        )
        for tile, low, high, at in pieces:
            here = slice(tile * 128, tile * 128 + 128)
            for k in range(low, high + 1):
                wt[kind, at + (k - low) * deep : at + (k - low + 1) * deep] = (
                    spread[:, here] * mask_ref[k : k + 1, here]
                ).astype(BF)

    def mix(kind, slot, m, left, chip=None):
        for tile, low, high, at in pieces:
            got = jnp.dot(
                left[:, low * deep : (high + 1) * deep],
                wt[kind, at : at + (high + 1 - low) * deep],
                preferred_element_type=F32,
            )
            u_buf[kind, slot, m, :, :, tile * 128 : tile * 128 + 128] = (
                got.reshape(groups, tall, 128).astype(BF)
            )
        block(kind, slot, m, chip).start()

    def settle(m):
        for d in range(1, nx):
            second(m, d).wait_recv()
        for y in range(tall):
            at = (y % share) * deep
            wf[pl.ds(y, a_rows, stride=tall), :] = w_land[m, y // share, :, at : at + deep].astype(F32)
        for k in range(a_in):
            part = jnp.concatenate(
                [wf[(g * a_in + k) * tall : (g * a_in + k + 1) * tall, :] for g in range(groups)], axis=0
            )
            w_own[m, :, k * deep : (k + 1) * deep] = part.astype(BF)

    def sketch():
        step = 16 if span % 16 == 0 else span
        along_x = east_ref[...].astype(F32)[None]
        part_x = jnp.zeros((rows, width), F32)
        part_z = jnp.zeros((deep, width), F32)
        for c in range(0, span, step):
            cells = f_buf[c : c + step].reshape(step * rows, deep)
            along_y = north_ref[c : c + step].astype(F32)[:, None, :]
            weighted = jnp.dot(cells, up_ref[...], preferred_element_type=F32).reshape(step, rows, width)
            p_buf[c : c + step] = jnp.sum(weighted * along_x, axis=1)
            part_x = part_x + jnp.sum(weighted * along_y, axis=0)
            khatri = (along_x * along_y).astype(BF).reshape(step * rows, width)
            part_z = part_z + lax.dot_general(
                cells, khatri, (((0,), (0,)), ((), ())), preferred_element_type=F32
            )
        for k in range(ny):
            q_buf[k, :x_rows] = part_x[k * x_rows : (k + 1) * x_rows]
            q_buf[k, x_rows:] = part_z[k * z_rows : (k + 1) * z_rows]

    def small(d):
        to = lax.rem(gy + d, ny)
        return send(q_buf.at[to], q_in.at[d], qs.at[d], qr.at[d], (gx, to))

    def small_y(d):
        to = lax.rem(gx + d, nx)
        return send(p_buf, y_in.at[d], ys.at[d], yr.at[d], (to, gy))

    def small_z(d):
        to = lax.rem(gx + d, nx)
        return send(z_own, z_in.at[d], zs.at[d], zr.at[d], (to, gy))

    def gather(d):
        to = lax.rem(gy + d, ny)
        return send(q_all.at[gy], q_all.at[gy], gs.at[d], gr.at[d], (gx, to))

    def gathered(d):
        source = lax.rem(gy - d + ny, ny)
        return send(q_all.at[source], q_all.at[source], gs.at[d], gr.at[d], (gx, source))

    def turn(c):
        loads[c].wait()
        t_buf[...] = n_buf[c].astype(F32).reshape(rows * batch, deep)
        for y in range(batch):
            f_buf[c * batch + y] = t_buf[pl.ds(y, rows, stride=batch), :].astype(BF)

    turn(0)
    send_first(0)
    send_first(1)
    early_sent = False
    for c in reversed(range(1, span // batch)):
        turn(c)
        if not early_sent and c * batch <= late * tall:
            early_sent = True

            @pl.when(middle)
            def _():
                for j in range(ahead):
                    early(j, 0).start()
                    early(j, 1).start()
    for copy in small_loads:
        copy.wait()
    sketch()
    for d in range(1, ny):
        small(d).start()
    for d in range(1, nx):
        small_y(d).start()
    mix_first(0)
    send_first(2)
    for kind in range(4):
        weigh(kind)

    done_y = pltpu.make_async_copy(fy_ref, fy_out, ds.at[0])

    def stage(s, carry):
        @pl.when(s + 1 < steps)
        def _():
            mix_first(s + 1)

        @pl.when(s + 3 < steps)
        def _():
            send_first(s + 3)

        @pl.when(s < steps)
        def _():
            settle(s)

        @pl.when(jnp.logical_and(s < steps, middle))
        def _():
            @pl.when(s < late)
            def _():
                raw(w_own.at[s], 1, s, last - spot).start()
                for kind in (2, 3):
                    mix(kind, 3, s, w_own.at[s])

        @pl.when(jnp.logical_and(s < steps, jnp.logical_not(middle)))
        def _():
            raw(w_own.at[s], 0, s, near).start()

        @pl.when(s < steps)
        def _():
            for kind in (1, 0):
                mix(kind, 3, s, w_own.at[s])

        @pl.when(s == 1)
        def _():
            for j in range(ahead):
                early(j, 1).wait_recv()
                send_first(steps + j)

        @pl.when(jnp.logical_and(s >= 2, s < 2 + ahead))
        def _():
            mix_first(steps + s - 2)

        @pl.when(jnp.logical_and(s >= 4, s < 4 + ahead))
        def _():
            settle(steps + s - 4)

        @pl.when(jnp.logical_and(jnp.logical_and(s >= 4, s < 4 + ahead), jnp.logical_not(middle)))
        def _():
            for kind in (1, 0):
                mix(kind, 0, late + s - 4, w_own.at[steps + s - 4], near)

        @pl.when(jnp.logical_and(jnp.logical_and(s >= 1, s < steps + 1), middle))
        def _():
            m = s - 1
            raw(w_own.at[m], 0, m, near).wait_recv()
            raw(w_in.at[0, m], 2, m, last - spot).start()

            @pl.when(m < late)
            def _():
                raw(w_own.at[m], 1, m, last - spot).wait_recv()
                for kind in (2, 3, 1, 0):
                    mix(kind, 1, m, w_in.at[1, m])

            @pl.when(m >= late)
            def _():
                for kind in (2, 3, 1, 0):
                    mix(kind, 1, m, w_own.at[m + ahead])

            for kind in (1, 0):
                mix(kind, 0, m, w_in.at[0, m])

        @pl.when(jnp.logical_and(s >= 2, middle))
        def _():
            m = s - 2
            raw(w_in.at[0, m], 2, m, last - spot).wait_recv()
            for kind in (2, 3, 1, 0):
                mix(kind, 2, m, w_in.at[2, m])

        @pl.when(s == 1)
        def _():
            for d in range(1, ny):
                small(d).wait()
            total = q_buf[gy]
            for d in range(1, ny):
                total = total + q_in[d]
            q_all[gy] = total
            z_own[...] = total[x_rows:]
            for d in range(1, nx):
                small_z(d).start()

        @pl.when(s == 3)
        def _():
            for d in range(1, nx):
                small_y(d).wait()
                small_z(d).wait()
            y_in[0] = p_buf[...]
            z_in[0] = z_own[...]
            y_total = jnp.zeros(p_buf.shape, F32)
            z_total = jnp.zeros(z_own.shape, F32)
            for g in range(nx):
                y_total = y_total + y_in[lax.rem(gx - g + nx, nx)]
                z_total = z_total + z_in[lax.rem(gx - g + nx, nx)]
            fy_ref[...] = y_total
            done_y.start()
            q_all[gy, x_rows:] = z_total
            for d in range(1, ny):
                gather(d).start()

        return carry

    lax.fori_loop(0, steps + 2, stage, 0)

    for d in range(1, ny):
        gather(d).wait_send()
        gathered(d).wait_recv()
    for k in range(ny):
        fx_ref[k * x_rows : (k + 1) * x_rows] = q_all[k, :x_rows]
        fz_ref[k * z_rows : (k + 1) * z_rows] = q_all[k, x_rows:]
    done_x = pltpu.make_async_copy(fx_ref, fx_out, ds.at[1])
    done_z = pltpu.make_async_copy(fz_ref, fz_out, ds.at[2])
    done_x.start()
    done_z.start()

    def close(m, carry):
        for d in range(1, nx):
            first(m, d).wait_send()
            second(m, d).wait_send()
        block(0, 3, m).wait()
        block(1, 3, m).wait_send()
        arrived(m, spot, 1 - core)

        @pl.when(middle)
        def _():
            raw(w_in.at[0, m], 2, m, last - spot).wait_send()

            @pl.when(m < late)
            def _():
                raw(w_own.at[m], 1, m, last - spot).wait_send()
                block(2, 3, m).wait_send()
                block(3, 3, m).wait_send()

            for slot in range(3):
                block(0, slot, m).wait()
                block(1, slot, m).wait_send()
                if slot:
                    block(2, slot, m).wait_send()
                    block(3, slot, m).wait_send()
                arrived(m, spots[slot], 1 - core)

        @pl.when(jnp.logical_not(middle))
        def _():
            raw(w_own.at[m], 0, m, near).wait_send()
            for d in range(1, ny // 2):
                for side in range(2):
                    at = lax.rem(spot + d, ny // 2)
                    here = jnp.logical_and(jnp.logical_and(at == near, side == core), m >= late)

                    @pl.when(jnp.logical_not(here))
                    def _(at=at, side=side):
                        arrived(m, at, side)

            @pl.when(m >= late)
            def _():
                block(0, 0, m, near).wait()
                block(1, 0, m, near).wait_send()

        return carry

    lax.fori_loop(0, steps, close, 0)
    for j in range(ahead):
        for d in range(1, nx):
            first(steps + j, d).wait_send()
            second(steps + j, d).wait_send()

    @pl.when(middle)
    def _():
        for j in range(ahead):
            early(j, 0).wait_send()
            early(j, 1).wait_send()

    for copy in (done_x, done_y, done_z):
        copy.wait()


def flow(field, gauss_east, gauss_up, east, north, up, nx, ny, a_in, lanes):
    rows, span, deep = field.shape
    a_rows = gauss_east.shape[0] // nx
    per_c = gauss_up.shape[0] // ny
    groups = a_rows // a_in
    tall = 8
    steps, share = span // tall, tall // nx
    ahead = 2
    most = steps + ahead
    width = up.shape[1]
    x_rows, z_rows = rows // ny, deep // ny
    lane = np.arange(lanes)
    used = lane < a_in * per_c
    sel = np.logical_and(lane[None] % per_c == np.arange(per_c)[:, None], used[None]).astype(np.float32)
    mask = (lane[None] // per_c == np.arange(a_in)[:, None]).astype(np.float32)
    total_k = sum(
        min((t * 128 + 127) // per_c, a_in - 1) + 1 - min(t * 128 // per_c, a_in - 1)
        for t in range(lanes // 128)
    ) * deep
    dma = lambda *shape: pltpu.SemaphoreType.DMA(shape)
    vm = pltpu.VMEM
    q_shape = (ny, x_rows + z_rows, width)
    batch = 16 if span % 16 == 0 else tall
    scratch = [
        vm((nx, a_rows, gauss_east.shape[1]), BF), vm(gauss_up.shape, BF), vm(sel.shape, BF),
        vm(mask.shape, F32), vm(east.shape, BF), vm(north.shape, BF), vm(up.shape, BF),
        vm((rows, width), F32), vm((deep, width), F32), vm((span, width), F32),
        vm((span // batch, rows, batch, deep), BF),
        vm((rows * batch, deep), F32),
        vm((span + ahead * tall, rows, deep), BF),
        vm((most, share, nx * rows, deep), BF),
        vm((most, nx - 1, a_rows, share * deep), BF),
        vm((most, nx, a_rows, share * deep), BF),
        vm((a_rows * tall, deep), F32),
        vm((most, groups * tall, a_in * deep), BF),
        vm((3, steps, groups * tall, a_in * deep), BF),
        vm((4, 4, steps, groups, tall, lanes), BF),
        vm((4, total_k, 128), BF),
        vm(q_shape, F32), vm(q_shape, F32), vm(q_shape, F32),
        vm((span, width), F32), vm((nx, span, width), F32),
        vm((nx, z_rows, width), F32), vm((z_rows, width), F32),
        dma(most, nx), dma(most, nx), dma(most), dma(most, nx), dma(most, nx),
        dma(2, ahead), dma(ahead),
        dma(3, steps), dma(3, steps), dma(4, 4, steps), dma(steps, ny // 2, 2), dma(4, steps),
        dma(span // batch), dma(7), dma(3),
        dma(ny), dma(ny), dma(nx), dma(nx), dma(nx), dma(nx), dma(ny), dma(ny),
    ]
    return pl.pallas_call(
        functools.partial(flow_kernel, nx, ny, per_c),
        out_shape=(
            pltpu.VMEM((groups, ny * span, lanes), BF),
            jax.ShapeDtypeStruct((rows, width), F32),
            jax.ShapeDtypeStruct((deep, width), F32),
            jax.ShapeDtypeStruct((span, width), F32),
        ),
        in_specs=[ANY] * 8,
        out_specs=(VMEM, ANY, ANY, ANY),
        scratch_shapes=scratch,
        compiler_params=pltpu.CompilerParams(collective_id=2, has_side_effects=True),
    )(
        field, gauss_east.reshape(nx, a_rows, -1), gauss_up,
        jnp.asarray(sel, BF), jnp.asarray(mask, F32), east, north, up,
    )


def mix_y_kernel(
    take, r_ref, g_ref, fx_ref, fy_ref, fz_ref, o_ref, fx_out, fy_out, fz_out,
    g_buf, o_buf, fx_buf, fy_buf, fz_buf, gs, os, fs, ts,
):
    groups = o_buf.shape[0]
    load = pltpu.make_async_copy(g_ref, g_buf, gs.at[0])
    load.start()
    trios = ((fx_ref, fx_buf, fx_out), (fy_ref, fy_buf, fy_out), (fz_ref, fz_buf, fz_out))
    ins = [pltpu.make_async_copy(src, mid, fs.at[k]) for k, (src, mid, _) in enumerate(trios)]
    stores = [pltpu.make_async_copy(mid, dst, ts.at[k]) for k, (_, mid, dst) in enumerate(trios)]
    for copy in ins:
        copy.start()
    load.wait()
    for c in range(0, groups, take):
        for k in range(c, c + take):
            o_buf[k] = lax.dot_general(
                r_ref[k], g_buf[...], (((0,), (1,)), ((), ())), preferred_element_type=F32
            )
        store = pltpu.make_async_copy(
            o_buf.at[pl.ds(c, take)], o_ref.at[pl.ds(c, take)], os.at[c // take]
        )
        store.start()
        stores.append(store)
        if c == 0:
            for k in range(3):
                ins[k].wait()
                stores[k].start()
    for copy in stores:
        copy.wait()


def mix_y(r, g, fx, fy, fz):
    groups, deep, lanes = r.shape
    out = g.shape[0]
    take = 1 if groups % 1 == 0 else 1
    dma = lambda *shape: pltpu.SemaphoreType.DMA(shape)
    vm = pltpu.VMEM
    like = lambda x: jax.ShapeDtypeStruct(x.shape, x.dtype)
    return pl.pallas_call(
        functools.partial(mix_y_kernel, take),
        out_shape=(jax.ShapeDtypeStruct((groups, lanes, out), F32), like(fx), like(fy), like(fz)),
        in_specs=[VMEM, ANY, ANY, ANY, ANY],
        out_specs=(ANY, ANY, ANY, ANY),
        scratch_shapes=[
            vm(g.shape, BF), vm((groups, lanes, out), F32), vm(fx.shape, F32), vm(fy.shape, F32),
            vm(fz.shape, F32), dma(1), dma(groups // take), dma(3), dma(3),
        ],
    )(r, g, fx, fy, fz)


def per_device(
    nx, ny,
    thermal_field,
    probe_range_east,
    probe_range_north,
    probe_range_upward,
    gauss_kernel_east,
    gauss_kernel_north,
    gauss_kernel_upward,
):
    rows, span, deep = thermal_field.shape
    a_rows = gauss_kernel_east.shape[0] // nx
    per_c = gauss_kernel_upward.shape[0] // ny
    a_in = 8 if a_rows % 8 == 0 and 8 * per_c % 128 == 0 else a_rows
    groups = a_rows // a_in
    used = a_in * per_c
    lanes = -(-used // 128) * 128

    if ny == 8 and 8 % nx == 0 and span % 8 == 0 and span // 8 > 5 and a_in % 8 == 0 and per_c % 16 == 0:
        r, factor_x, factor_z, factor_y = flow(
            thermal_field, gauss_kernel_east, gauss_kernel_upward,
            probe_range_east, probe_range_north, probe_range_upward, nx, ny, a_in, lanes,
        )
        r = pltpu.with_memory_space_constraint(r, pltpu.VMEM)
    else:
        w, q, part_y = mix_x(
            thermal_field.reshape(rows, span * deep),
            gauss_kernel_east.reshape(nx, a_rows, -1),
            nx,
            a_rows,
            thermal_field,
            probe_range_east,
            probe_range_north,
            probe_range_upward,
            ny,
        )
        w = w.reshape(groups, a_in, span, deep).transpose(0, 2, 1, 3).reshape(groups * span, a_in * deep)

        gt = gauss_kernel_upward.reshape(ny, per_c, deep).transpose(0, 2, 1)
        gt = jnp.pad(jnp.tile(gt, (1, 1, a_in)), ((0, 0), (0, 0), (0, lanes - used)))
        mask = (
            lax.broadcasted_iota(jnp.int32, (a_in, lanes), 1) // per_c
            == lax.broadcasted_iota(jnp.int32, (a_in, lanes), 0)
        ).astype(BF)
        r, factor_x, factor_z, factor_y = exchange(w, gt, mask, q, part_y, nx, ny, groups, span, per_c)

    core, factor_x, factor_y, factor_z = mix_y(r, gauss_kernel_north, factor_x, factor_y, factor_z)
    core = core[:, :used].reshape(a_rows, per_c, -1).transpose(0, 2, 1)
    return (factor_x, factor_y, factor_z, core)


def solution(mesh):
    in_specs = (P("gx", "gy", None), P("gx", None), P("gy", None), P(), P(), P(), P())
    out_specs = (P("gx", None), P("gy", None), P(), P("gx", None, "gy"))
    body = functools.partial(per_device, mesh.shape["gx"], mesh.shape["gy"])
    return jax.shard_map(
        body, mesh=mesh, in_specs=in_specs, out_specs=out_specs, check_vma=False
    )
```

```python
import functools

import jax
import jax.numpy as jnp
import numpy as np
from jax import lax
from jax.experimental import pallas as pl
from jax.experimental.pallas import tpu as pltpu
from jax.sharding import PartitionSpec as P

MESH = pl.DeviceIdType.MESH
VMEM = pl.BlockSpec(memory_space=pltpu.VMEM)
ANY = pl.BlockSpec(memory_space=pl.ANY)
BF = jnp.bfloat16
F32 = jnp.float32


def remote(src, dst, send, recv, where):
    copy = pltpu.make_async_remote_copy(
        src_ref=src, dst_ref=dst, send_sem=send, recv_sem=recv, device_id=where, device_id_type=MESH
    )
    copy.start()
    return copy


def sketch_parts(f_ref, east_ref, north_ref, up_ref, q_ref, py_ref, px_buf):
    rows, span, deep = f_ref.shape
    width = up_ref.shape[1]
    step = 16 if rows % 16 == 0 else rows
    along_y = north_ref[...].astype(F32)
    part_y = jnp.zeros((span, width), F32)
    part_z = jnp.zeros((deep, width), F32)
    for c in range(0, rows, step):
        cells = f_ref[c : c + step].reshape(step * span, deep)
        along_x = east_ref[c : c + step].astype(F32)
        weighted = jnp.dot(cells, up_ref[...], preferred_element_type=F32).reshape(step, span, width)
        px_buf[c : c + step] = jnp.sum(weighted * along_y[None, :, :], axis=1)
        part_y = part_y + jnp.sum(weighted * along_x[:, None, :], axis=0)
        khatri = (along_x[:, None, :] * along_y[None, :, :]).astype(BF).reshape(step * span, width)
        part_z = part_z + lax.dot_general(
            cells, khatri, (((0,), (0,)), ((), ())), preferred_element_type=F32
        )
    py_ref[...] = part_y
    ny = q_ref.shape[0]
    x_rows, z_rows = rows // ny, deep // ny
    for k in range(ny):
        q_ref[k, :x_rows] = px_buf[k * x_rows : (k + 1) * x_rows]
        q_ref[k, x_rows:] = part_z[k * z_rows : (k + 1) * z_rows]


def mix_x_kernel(
    n, chunks, t_ref, g_ref, f_ref, east_ref, north_ref, up_ref, w_ref, q_ref, py_ref,
    x_buf, y_buf, px_buf, s1, r1, s2, r2, ls,
):
    gx, gy = lax.axis_index("gx"), lax.axis_index("gy")
    rows = t_ref.shape[0]
    a_rows = y_buf.shape[2]
    wide = t_ref.shape[1] // n
    part = wide // chunks
    barrier = pltpu.get_barrier_semaphore()
    for d in range(1, n):
        pl.semaphore_signal(barrier, inc=1, device_id=(lax.rem(gx + d, n), gy), device_id_type=MESH)
    pl.semaphore_wait(barrier, n - 1)

    first, second, local = [], [], []
    for m in range(chunks):
        for d in range(1, n):
            to = lax.rem(gx + d, n)
            lanes = pl.ds(pl.multiple_of(to * wide + m * part, 128), part)
            first.append(
                remote(t_ref.at[:, lanes], x_buf.at[m, gx], s1.at[m, d], r1.at[m, d], (to, gy))
            )
        lanes = pl.ds(pl.multiple_of(gx * wide + m * part, 128), part)
        own = pltpu.make_async_copy(t_ref.at[:, lanes], x_buf.at[m, gx], ls.at[m, 0])
        own.start()
        local.append(own)
    sketch_parts(f_ref, east_ref, north_ref, up_ref, q_ref, py_ref, px_buf)
    for m in range(chunks):
        local[m].wait()
        for d in range(1, n):
            first[m * (n - 1) + d - 1].wait()
        block = x_buf[m].reshape(n * rows, part)
        lanes = pl.ds(pl.multiple_of(gx * wide + m * part, 128), part)
        for d in range(1, n + 1):
            to = lax.rem(gx + d, n)
            y_buf[m, d - 1] = jnp.dot(g_ref[to], block, preferred_element_type=F32).astype(BF)
            if d < n:
                second.append(
                    remote(
                        y_buf.at[m, d - 1], w_ref.at[:, lanes], s2.at[m, d], r2.at[m, d], (to, gy)
                    )
                )
            else:
                own = pltpu.make_async_copy(y_buf.at[m, d - 1], w_ref.at[:, lanes], ls.at[m, 1])
                own.start()
                second.append(own)
    for copy in second:
        copy.wait()


def mix_x(field, gauss, n, a_rows, cells, east, north, up, ny):
    rows, lanes = field.shape
    wide = lanes // n
    chunks = 3 if wide % 384 == 0 else 1
    dma = lambda *shape: pltpu.SemaphoreType.DMA(shape)
    return pl.pallas_call(
        functools.partial(mix_x_kernel, n, chunks),
        out_shape=(
            jax.ShapeDtypeStruct((a_rows, lanes), BF),
            jax.ShapeDtypeStruct((ny, (cells.shape[0] + cells.shape[2]) // ny, up.shape[1]), F32),
            jax.ShapeDtypeStruct(north.shape, F32),
        ),
        in_specs=[VMEM] * 6,
        out_specs=(VMEM, VMEM, VMEM),
        scratch_shapes=[
            pltpu.VMEM((chunks, n, rows, wide // chunks), BF),
            pltpu.VMEM((chunks, n, a_rows, wide // chunks), BF),
            pltpu.VMEM(east.shape, F32),
            dma(chunks, n), dma(chunks, n), dma(chunks, n), dma(chunks, n), dma(chunks, 2),
        ],
        compiler_params=pltpu.CompilerParams(collective_id=0, has_side_effects=True),
    )(field, gauss, cells, east, north, up)


def exchange_kernel(
    nx, ny, batches, per_c, w_ref, gt_ref, mask_ref, q_ref, py_ref,
    r_ref, fx_ref, fz_ref, pyo_ref,
    u_buf, q_in, q_all, y_in, z_in, z_own,
    us, ur, ul, qs, qr, ys, yr, zs, zr, gs, gr,
):
    gx, gy = lax.axis_index("gx"), lax.axis_index("gy")
    span = u_buf.shape[3]
    per = u_buf.shape[2]
    lanes = u_buf.shape[4]
    a_in = mask_ref.shape[0]
    deep = gt_ref.shape[1]
    x_rows = q_ref.shape[1] - z_in.shape[1]
    barrier = pltpu.get_barrier_semaphore()
    for d in range(1, ny):
        pl.semaphore_signal(barrier, inc=1, device_id=(gx, lax.rem(gy + d, ny)), device_id_type=MESH)
    for d in range(1, nx):
        pl.semaphore_signal(barrier, inc=1, device_id=(lax.rem(gx + d, nx), gy), device_id_type=MESH)
    pl.semaphore_wait(barrier, nx + ny - 2)

    small, ysmall, big = [], [], []
    for d in range(1, ny):
        to = lax.rem(gy + d, ny)
        small.append(remote(q_ref.at[to], q_in.at[d], qs.at[d], qr.at[d], (gx, to)))
    for d in range(1, nx):
        to = lax.rem(gx + d, nx)
        ysmall.append(remote(py_ref, y_in.at[d], ys.at[d], yr.at[d], (to, gy)))

    rows_b = per * span
    for b in range(batches):
        for d in range(1, ny + 1):
            to = lax.rem(gy + d, ny)
            for tile in range(lanes // 128):
                low = min(tile * 128 // per_c, a_in - 1)
                high = min((tile * 128 + 127) // per_c, a_in - 1)
                here = slice(tile * 128, tile * 128 + 128)
                weights = jnp.concatenate(
                    [gt_ref[to, :, here] * mask_ref[k : k + 1, here] for k in range(low, high + 1)], axis=0
                )
                left = w_ref[b * rows_b : (b + 1) * rows_b, low * deep : (high + 1) * deep]
                got = jnp.dot(left, weights, preferred_element_type=F32).astype(BF)
                u_buf[b, d - 1, :, :, here] = got.reshape(per, span, 128)
            target = r_ref.at[pl.ds(b * per, per), pl.ds(pl.multiple_of(gy * span, span), span), :]
            if d < ny:
                big.append(remote(u_buf.at[b, d - 1], target, us.at[b, d], ur.at[b, d], (gx, to)))
            else:
                own = pltpu.make_async_copy(u_buf.at[b, d - 1], target, ul.at[b])
                own.start()
                big.append(own)
        if b == 0:
            for copy in small:
                copy.wait()
            total = q_ref[gy]
            for d in range(1, ny):
                total = total + q_in[d]
            z_own[...] = total[x_rows:]
            zsmall = []
            for d in range(1, nx):
                to = lax.rem(gx + d, nx)
                zsmall.append(remote(z_own, z_in.at[d], zs.at[d], zr.at[d], (to, gy)))
            for copy in ysmall:
                copy.wait()
            y_in[0] = py_ref[...]
            y_total = jnp.zeros(py_ref.shape, F32)
            for g in range(nx):
                y_total = y_total + y_in[lax.rem(gx - g + nx, nx)]
            pyo_ref[...] = y_total
    for copy in zsmall:
        copy.wait()
    z_in[0] = z_own[...]
    z_total = jnp.zeros(z_own.shape, F32)
    for g in range(nx):
        z_total = z_total + z_in[lax.rem(gx - g + nx, nx)]
    q_all[gy, :x_rows] = total[:x_rows]
    q_all[gy, x_rows:] = z_total
    gathers = []
    for d in range(1, ny):
        to = lax.rem(gy + d, ny)
        gathers.append(remote(q_all.at[gy], q_all.at[gy], gs.at[d], gr.at[d], (gx, to)))
    for copy in gathers:
        copy.wait()
    z_rows = z_own.shape[0]
    for k in range(ny):
        fx_ref[k * x_rows : (k + 1) * x_rows] = q_all[k, :x_rows]
        fz_ref[k * z_rows : (k + 1) * z_rows] = q_all[k, x_rows:]
    for copy in big:
        copy.wait()


def line_kernel(
    nx, ny, batches, per_c, w_ref, gt_ref, mask_ref, q_ref, py_ref,
    r_ref, fx_ref, fz_ref, pyo_ref,
    w_in, u_buf, wt, q_in, q_all, y_in, z_in, z_own,
    ws, wr, us, ur, ul, qs, qr, ys, yr, zs, zr, gs, gr,
):
    gx, gy = lax.axis_index("gx"), lax.axis_index("gy")
    spot, core = gy // 2, gy % 2
    last = ny // 2 - 1
    middle = jnp.logical_and(spot > 0, spot < last)
    left_half = spot * 2 < last
    end = jnp.where(left_half, 0, last)
    near = jnp.where(left_half, 1, last - 1)
    _, _, _, per, span, lanes = u_buf.shape
    a_in = mask_ref.shape[0]
    deep = gt_ref.shape[1]
    x_rows = q_ref.shape[1] - z_in.shape[1]
    rows_b = per * span
    spots = (end, last - spot, last - end, spot)
    goals = (gy, 2 * spot + 1 - core, 2 * end, 2 * end + 1)
    barrier = pltpu.get_barrier_semaphore()
    for d in range(1, ny):
        pl.semaphore_signal(barrier, inc=1, device_id=(gx, lax.rem(gy + d, ny)), device_id_type=MESH)
    for d in range(1, nx):
        pl.semaphore_signal(barrier, inc=1, device_id=(lax.rem(gx + d, nx), gy), device_id_type=MESH)
    pl.semaphore_wait(barrier, nx + ny - 2)

    small, ysmall = [], []
    for d in range(1, ny):
        to = lax.rem(gy + d, ny)
        small.append(remote(q_ref.at[to], q_in.at[d], qs.at[d], qr.at[d], (gx, to)))
    for d in range(1, nx):
        to = lax.rem(gx + d, nx)
        ysmall.append(remote(py_ref, y_in.at[d], ys.at[d], yr.at[d], (to, gy)))

    def raw(src, slot, b, to_spot):
        return pltpu.make_async_remote_copy(
            src_ref=src, dst_ref=w_in.at[slot, b], send_sem=ws.at[slot, b], recv_sem=wr.at[slot, b],
            device_id=(gx, 2 * to_spot + core), device_id_type=MESH,
        )

    def rows_of(b):
        return w_ref.at[pl.ds(b * rows_b, rows_b), :]

    def place(b, origin):
        return r_ref.at[pl.ds(b * per, per), pl.ds(pl.multiple_of(origin * span, span), span), :]

    def block(kind, slot, b):
        source = 2 * spots[slot] + core
        if kind == 0:
            return pltpu.make_async_copy(u_buf.at[kind, slot, b], place(b, source), ul.at[slot, b])
        return pltpu.make_async_remote_copy(
            src_ref=u_buf.at[kind, slot, b], dst_ref=place(b, source),
            send_sem=us.at[kind, slot, b], recv_sem=ur.at[b, spots[slot], core],
            device_id=(gx, goals[kind]), device_id_type=MESH,
        )

    def arrived(b, at, side):
        pltpu.make_async_remote_copy(
            src_ref=u_buf.at[0, 0, b], dst_ref=place(b, 2 * at + side),
            send_sem=us.at[1, 0, b], recv_sem=ur.at[b, at, side],
            device_id=(gx, goals[1]), device_id_type=MESH,
        ).wait_recv()

    pieces, base = [], 0
    for tile in range(lanes // 128):
        low = min(tile * 128 // per_c, a_in - 1)
        high = min((tile * 128 + 127) // per_c, a_in - 1)
        pieces.append((tile, low, high, base))
        base += (high + 1 - low) * deep

    def weigh(kind):
        for tile, low, high, at in pieces:
            here = slice(tile * 128, tile * 128 + 128)
            for k in range(low, high + 1):
                wt[kind, at + (k - low) * deep : at + (k - low + 1) * deep] = (
                    gt_ref[goals[kind], :, here] * mask_ref[k : k + 1, here]
                )

    def mix(kind, slot, b, left):
        for tile, low, high, at in pieces:
            got = jnp.dot(
                left[:, low * deep : (high + 1) * deep],
                wt[kind, at : at + (high + 1 - low) * deep],
                preferred_element_type=F32,
            ).astype(BF)
            u_buf[kind, slot, b, :, :, tile * 128 : tile * 128 + 128] = got.reshape(per, span, 128)

    def own_blocks(kind):
        weigh(kind)
        for b in range(batches):
            mix(kind, 3, b, rows_of(b))
            block(kind, 3, b).start()

    @pl.when(middle)
    def _():
        for b in range(batches):
            raw(rows_of(b), 1, b, last - spot).start()
        for kind in (2, 3):
            own_blocks(kind)

    @pl.when(jnp.logical_not(middle))
    def _():
        for b in range(batches):
            raw(rows_of(b), 0, b, near).start()

    for kind in (1, 0):
        own_blocks(kind)

    for copy in small:
        copy.wait()
    total = q_ref[gy]
    for d in range(1, ny):
        total = total + q_in[d]
    z_own[...] = total[x_rows:]
    zsmall = []
    for d in range(1, nx):
        to = lax.rem(gx + d, nx)
        zsmall.append(remote(z_own, z_in.at[d], zs.at[d], zr.at[d], (to, gy)))
    for copy in ysmall:
        copy.wait()
    y_in[0] = py_ref[...]
    y_total = jnp.zeros(py_ref.shape, F32)
    for g in range(nx):
        y_total = y_total + y_in[lax.rem(gx - g + nx, nx)]
    pyo_ref[...] = y_total
    for copy in zsmall:
        copy.wait()
    z_in[0] = z_own[...]
    z_total = jnp.zeros(z_own.shape, F32)
    for g in range(nx):
        z_total = z_total + z_in[lax.rem(gx - g + nx, nx)]
    q_all[gy, :x_rows] = total[:x_rows]
    q_all[gy, x_rows:] = z_total
    gathers = []
    for d in range(1, ny):
        to = lax.rem(gy + d, ny)
        gathers.append(remote(q_all.at[gy], q_all.at[gy], gs.at[d], gr.at[d], (gx, to)))

    @pl.when(middle)
    def _():
        for b in range(batches):
            raw(rows_of(b), 0, b, near).wait_recv()
            raw(w_in.at[0, b], 2, b, last - spot).start()
            raw(rows_of(b), 1, b, last - spot).wait_recv()
            for kind, slot in ((2, 1), (3, 1), (1, 1), (1, 0), (0, 1), (0, 0)):
                mix(kind, slot, b, w_in.at[slot, b])
                block(kind, slot, b).start()
        for b in range(batches):
            raw(w_in.at[0, b], 2, b, last - spot).wait_recv()
            for kind in (2, 3, 1, 0):
                mix(kind, 2, b, w_in.at[2, b])
                block(kind, 2, b).start()
        for b in range(batches):
            raw(rows_of(b), 1, b, last - spot).wait_send()
            raw(w_in.at[0, b], 2, b, last - spot).wait_send()
            for slot in range(4):
                block(0, slot, b).wait()
                block(1, slot, b).wait_send()
                if slot:
                    block(2, slot, b).wait_send()
                    block(3, slot, b).wait_send()
                arrived(b, spots[slot], 1 - core)

    @pl.when(jnp.logical_not(middle))
    def _():
        for b in range(batches):
            raw(rows_of(b), 0, b, near).wait_send()
            block(0, 3, b).wait()
            block(1, 3, b).wait_send()
            arrived(b, spot, 1 - core)
            for d in range(1, ny // 2):
                for side in range(2):
                    arrived(b, lax.rem(spot + d, ny // 2), side)

    for copy in gathers:
        copy.wait()
    z_rows = z_own.shape[0]
    for k in range(ny):
        fx_ref[k * x_rows : (k + 1) * x_rows] = q_all[k, :x_rows]
        fz_ref[k * z_rows : (k + 1) * z_rows] = q_all[k, x_rows:]


def exchange(w, gt, mask, q, py, nx, ny, groups, span, per_c):
    lanes = gt.shape[2]
    deep = gt.shape[1]
    z_rows = deep // ny
    dma = lambda *shape: pltpu.SemaphoreType.DMA(shape)
    vm = pltpu.VMEM
    sums = [
        vm(q.shape, F32), vm(q.shape, F32), vm((nx,) + py.shape, F32),
        vm((nx, z_rows, q.shape[2]), F32), vm((z_rows, q.shape[2]), F32),
    ]
    sum_sems = [dma(ny), dma(ny), dma(nx), dma(nx), dma(nx), dma(nx), dma(ny), dma(ny)]
    if ny == 8 and groups % 4 == 0:
        batches = 4
        per = groups // batches
        total_k = sum(
            min((t * 128 + 127) // per_c, mask.shape[0] - 1) + 1 - t * 128 // per_c
            for t in range(lanes // 128)
        ) * deep
        body = functools.partial(line_kernel, nx, ny, batches, per_c)
        scratch = [
            vm((3, batches, per * span, w.shape[1]), BF),
            vm((4, 4, batches, per, span, lanes), BF),
            vm((4, total_k, 128), BF),
        ] + sums + [
            dma(3, batches), dma(3, batches), dma(4, 4, batches), dma(batches, ny // 2, 2),
            dma(4, batches),
        ] + sum_sems
    else:
        batches = 3 if groups % 3 == 0 else 1
        per = groups // batches
        body = functools.partial(exchange_kernel, nx, ny, batches, per_c)
        scratch = [vm((batches, ny, per, span, lanes), BF)] + sums + [
            dma(batches, ny), dma(batches, ny), dma(batches)
        ] + sum_sems
    return pl.pallas_call(
        body,
        out_shape=(
            jax.ShapeDtypeStruct((groups, ny * span, lanes), BF),
            jax.ShapeDtypeStruct((ny * q.shape[1] - deep, q.shape[2]), F32),
            jax.ShapeDtypeStruct((deep, q.shape[2]), F32),
            jax.ShapeDtypeStruct(py.shape, F32),
        ),
        in_specs=[VMEM] * 5,
        out_specs=(ANY, VMEM, VMEM, VMEM),
        scratch_shapes=scratch,
        compiler_params=pltpu.CompilerParams(collective_id=1, has_side_effects=True),
    )(w, gt, mask, q, py)


def flow_kernel(
    nx, ny, per_c, field, gauss, gauss_up, select, masks, east, north, up,
    r_ref, fx_out, fz_out, fy_out,
    g_ref, gu_ref, sel_ref, mask_ref, east_ref, north_ref, up_ref, fx_ref, fz_ref, fy_ref,
    n_buf, t_buf, f_buf, x_buf, y_buf, w_land, wf, w_own, w_in, u_buf, wt,
    q_buf, q_in, q_all, p_buf, y_in, z_in, z_own,
    s1, r1, l1, s2, r2, ps, pr, ws, wr, us, ur, ul, fs, os, ds, qs, qr, ys, yr, zs, zr, gs, gr,
):
    gx, gy = lax.axis_index("gx"), lax.axis_index("gy")
    spot, core = gy // 2, gy % 2
    last = ny // 2 - 1
    middle = jnp.logical_and(spot > 0, spot < last)
    left_half = spot * 2 < last
    end = jnp.where(left_half, 0, last)
    near = jnp.where(left_half, 1, last - 1)
    spots = (end, last - spot, last - end, spot)
    goals = (gy, 2 * spot + 1 - core, 2 * end, 2 * end + 1)

    _, rows, deep = f_buf.shape
    share = x_buf.shape[1]
    span = north_ref.shape[0]
    _, _, steps, groups, tall, lanes = u_buf.shape
    ahead = x_buf.shape[0] - steps
    late = steps - ahead
    a_in = mask_ref.shape[0]
    a_rows = groups * a_in
    width = up_ref.shape[1]
    x_rows, z_rows = rows // ny, deep // ny

    batch = n_buf.shape[2]
    loads = [
        pltpu.make_async_copy(field.at[:, c * batch : (c + 1) * batch, :], n_buf.at[c], fs.at[c])
        for c in range(span // batch)
    ]
    for copy in loads:
        copy.start()
    small_loads = [
        pltpu.make_async_copy(src, dst, os.at[k])
        for k, (src, dst) in enumerate(
            (
                (east, east_ref), (north, north_ref), (up, up_ref), (gauss, g_ref),
                (gauss_up, gu_ref), (select, sel_ref), (masks, mask_ref),
            )
        )
    ]
    for copy in small_loads:
        copy.start()
    barrier = pltpu.get_barrier_semaphore()
    for d in range(1, ny):
        pl.semaphore_signal(barrier, inc=1, device_id=(gx, lax.rem(gy + d, ny)), device_id_type=MESH)
    for d in range(1, nx):
        pl.semaphore_signal(barrier, inc=1, device_id=(lax.rem(gx + d, nx), gy), device_id_type=MESH)

    def turn(c):
        loads[c].wait()
        t_buf[...] = n_buf[c].astype(F32).reshape(rows * batch, deep)
        for y in range(batch):
            f_buf[c * batch + y] = t_buf[pl.ds(y, rows, stride=batch), :].astype(BF)

    turn(0)
    pl.semaphore_wait(barrier, nx + ny - 2)

    def send(src, dst, ssem, rsem, where):
        return pltpu.make_async_remote_copy(
            src_ref=src, dst_ref=dst, send_sem=ssem, recv_sem=rsem, device_id=where, device_id_type=MESH
        )

    def first(m, d):
        to = lax.rem(gx + d, nx)
        src = f_buf.at[pl.ds(m * tall + to * share, share)]
        dst = x_buf.at[m, :, pl.ds(pl.multiple_of(gx * rows, rows), rows), :]
        if d == nx:
            return pltpu.make_async_copy(src, dst, l1.at[m])
        return send(src, dst, s1.at[m, d], r1.at[m, d], (to, gy))

    def second(m, d):
        to = lax.rem(gx + d, nx)
        return send(y_buf.at[m, d - 1], w_land.at[m, gx], s2.at[m, d], r2.at[m, d], (to, gy))

    def early(j, way):
        to = jnp.where(way == 0, end, last - spot)
        return send(
            f_buf.at[pl.ds((late + j) * tall, tall)], f_buf.at[pl.ds(span + j * tall, tall)],
            ps.at[way, j], pr.at[j], (gx, 2 * to + core),
        )

    def send_first(m):
        for d in range(1, nx + 1):
            first(m, d).start()

    def mix_first(m):
        first(m, nx).wait()
        for d in range(1, nx):
            first(m, d).wait_recv()
        block = jnp.concatenate([x_buf[m, j] for j in range(share)], axis=1)
        for d in range(1, nx + 1):
            to = lax.rem(gx + d, nx)
            got = jnp.dot(g_ref[to], block, preferred_element_type=F32).astype(BF)
            if d < nx:
                y_buf[m, d - 1] = got
                second(m, d).start()
            else:
                w_land[m, gx] = got

    def raw(src, slot, m, to_spot):
        return send(src, w_in.at[slot, m], ws.at[slot, m], wr.at[slot, m], (gx, 2 * to_spot + core))

    def place(m, origin):
        return r_ref.at[:, pl.ds(pl.multiple_of(origin * span + m * tall, tall), tall), :]

    def block(kind, slot, m, chip=None):
        chip = spots[slot] if chip is None else chip
        source = 2 * chip + core
        if kind == 0:
            return pltpu.make_async_copy(u_buf.at[kind, slot, m], place(m, source), ul.at[slot, m])
        return send(
            u_buf.at[kind, slot, m], place(m, source), us.at[kind, slot, m],
            ur.at[m, chip, core], (gx, goals[kind]),
        )

    def arrived(m, at, side):
        send(
            u_buf.at[0, 0, m], place(m, 2 * at + side), us.at[1, 0, m], ur.at[m, at, side], (gx, goals[1])
        ).wait_recv()

    pieces, base = [], 0
    for tile in range(lanes // 128):
        low = min(tile * 128 // per_c, a_in - 1)
        high = min((tile * 128 + 127) // per_c, a_in - 1)
        pieces.append((tile, low, high, base))
        base += (high + 1 - low) * deep

    def weigh(kind):
        mine = gu_ref[pl.ds(pl.multiple_of(goals[kind] * per_c, per_c), per_c), :]
        spread = lax.dot_general(
            mine, sel_ref[...], (((0,), (0,)), ((), ())), preferred_element_type=F32
        )
        for tile, low, high, at in pieces:
            here = slice(tile * 128, tile * 128 + 128)
            for k in range(low, high + 1):
                wt[kind, at + (k - low) * deep : at + (k - low + 1) * deep] = (
                    spread[:, here] * mask_ref[k : k + 1, here]
                ).astype(BF)

    def mix(kind, slot, m, left, chip=None):
        for tile, low, high, at in pieces:
            got = jnp.dot(
                left[:, low * deep : (high + 1) * deep],
                wt[kind, at : at + (high + 1 - low) * deep],
                preferred_element_type=F32,
            )
            u_buf[kind, slot, m, :, :, tile * 128 : tile * 128 + 128] = (
                got.reshape(groups, tall, 128).astype(BF)
            )
        block(kind, slot, m, chip).start()

    def settle(m):
        for d in range(1, nx):
            second(m, d).wait_recv()
        for y in range(tall):
            at = (y % share) * deep
            wf[pl.ds(y, a_rows, stride=tall), :] = w_land[m, y // share, :, at : at + deep].astype(F32)
        for k in range(a_in):
            part = jnp.concatenate(
                [wf[(g * a_in + k) * tall : (g * a_in + k + 1) * tall, :] for g in range(groups)], axis=0
            )
            w_own[m, :, k * deep : (k + 1) * deep] = part.astype(BF)

    def sketch():
        step = 16 if span % 16 == 0 else span
        along_x = east_ref[...].astype(F32)[None]
        part_x = jnp.zeros((rows, width), F32)
        part_z = jnp.zeros((deep, width), F32)
        for c in range(0, span, step):
            cells = f_buf[c : c + step].reshape(step * rows, deep)
            along_y = north_ref[c : c + step].astype(F32)[:, None, :]
            weighted = jnp.dot(cells, up_ref[...], preferred_element_type=F32).reshape(step, rows, width)
            p_buf[c : c + step] = jnp.sum(weighted * along_x, axis=1)
            part_x = part_x + jnp.sum(weighted * along_y, axis=0)
            khatri = (along_x * along_y).astype(BF).reshape(step * rows, width)
            part_z = part_z + lax.dot_general(
                cells, khatri, (((0,), (0,)), ((), ())), preferred_element_type=F32
            )
        for k in range(ny):
            q_buf[k, :x_rows] = part_x[k * x_rows : (k + 1) * x_rows]
            q_buf[k, x_rows:] = part_z[k * z_rows : (k + 1) * z_rows]

    def small(d):
        to = lax.rem(gy + d, ny)
        return send(q_buf.at[to], q_in.at[d], qs.at[d], qr.at[d], (gx, to))

    def small_y(d):
        to = lax.rem(gx + d, nx)
        return send(p_buf, y_in.at[d], ys.at[d], yr.at[d], (to, gy))

    def small_z(d):
        to = lax.rem(gx + d, nx)
        return send(z_own, z_in.at[d], zs.at[d], zr.at[d], (to, gy))

    def gather(d):
        to = lax.rem(gy + d, ny)
        return send(q_all.at[gy], q_all.at[gy], gs.at[d], gr.at[d], (gx, to))

    def gathered(d):
        source = lax.rem(gy - d + ny, ny)
        return send(q_all.at[source], q_all.at[source], gs.at[d], gr.at[d], (gx, source))

    send_first(0)
    send_first(1)
    early_sent = False
    for c in reversed(range(1, span // batch)):
        turn(c)
        if not early_sent and c * batch <= late * tall:
            early_sent = True

            @pl.when(middle)
            def _():
                for j in range(ahead):
                    early(j, 0).start()
                    early(j, 1).start()
    for copy in small_loads:
        copy.wait()
    sketch()
    for d in range(1, ny):
        small(d).start()
    for d in range(1, nx):
        small_y(d).start()
    mix_first(0)
    send_first(2)
    for kind in range(4):
        weigh(kind)

    done_y = pltpu.make_async_copy(fy_ref, fy_out, ds.at[0])

    def stage(s, carry):
        @pl.when(s + 1 < steps)
        def _():
            mix_first(s + 1)

        @pl.when(s + 3 < steps)
        def _():
            send_first(s + 3)

        @pl.when(s < steps)
        def _():
            settle(s)

        @pl.when(jnp.logical_and(s < steps, middle))
        def _():
            @pl.when(s < late)
            def _():
                raw(w_own.at[s], 1, s, last - spot).start()
                for kind in (2, 3):
                    mix(kind, 3, s, w_own.at[s])

        @pl.when(jnp.logical_and(s < steps, jnp.logical_not(middle)))
        def _():
            raw(w_own.at[s], 0, s, near).start()

        @pl.when(s < steps)
        def _():
            for kind in (1, 0):
                mix(kind, 3, s, w_own.at[s])

        @pl.when(s == 1)
        def _():
            for j in range(ahead):
                early(j, 1).wait_recv()
                send_first(steps + j)

        @pl.when(jnp.logical_and(s >= 2, s < 2 + ahead))
        def _():
            mix_first(steps + s - 2)

        @pl.when(jnp.logical_and(s >= 4, s < 4 + ahead))
        def _():
            settle(steps + s - 4)

        @pl.when(jnp.logical_and(jnp.logical_and(s >= 4, s < 4 + ahead), jnp.logical_not(middle)))
        def _():
            for kind in (1, 0):
                mix(kind, 0, late + s - 4, w_own.at[steps + s - 4], near)

        @pl.when(jnp.logical_and(jnp.logical_and(s >= 1, s < steps + 1), middle))
        def _():
            m = s - 1
            raw(w_own.at[m], 0, m, near).wait_recv()
            raw(w_in.at[0, m], 2, m, last - spot).start()

            @pl.when(m < late)
            def _():
                raw(w_own.at[m], 1, m, last - spot).wait_recv()
                for kind in (2, 3, 1, 0):
                    mix(kind, 1, m, w_in.at[1, m])

            @pl.when(m >= late)
            def _():
                for kind in (2, 3, 1, 0):
                    mix(kind, 1, m, w_own.at[m + ahead])

            for kind in (1, 0):
                mix(kind, 0, m, w_in.at[0, m])

        @pl.when(jnp.logical_and(s >= 2, middle))
        def _():
            m = s - 2
            raw(w_in.at[0, m], 2, m, last - spot).wait_recv()
            for kind in (2, 3, 1, 0):
                mix(kind, 2, m, w_in.at[2, m])

        @pl.when(s == 1)
        def _():
            for d in range(1, ny):
                small(d).wait()
            total = q_buf[gy]
            for d in range(1, ny):
                total = total + q_in[d]
            q_all[gy] = total
            z_own[...] = total[x_rows:]
            for d in range(1, nx):
                small_z(d).start()

        @pl.when(s == 3)
        def _():
            for d in range(1, nx):
                small_y(d).wait()
                small_z(d).wait()
            y_in[0] = p_buf[...]
            z_in[0] = z_own[...]
            y_total = jnp.zeros(p_buf.shape, F32)
            z_total = jnp.zeros(z_own.shape, F32)
            for g in range(nx):
                y_total = y_total + y_in[lax.rem(gx - g + nx, nx)]
                z_total = z_total + z_in[lax.rem(gx - g + nx, nx)]
            fy_ref[...] = y_total
            done_y.start()
            q_all[gy, x_rows:] = z_total
            for d in range(1, ny):
                gather(d).start()

        return carry

    lax.fori_loop(0, steps + 2, stage, 0)

    for d in range(1, ny):
        gather(d).wait_send()
        gathered(d).wait_recv()
    for k in range(ny):
        fx_ref[k * x_rows : (k + 1) * x_rows] = q_all[k, :x_rows]
        fz_ref[k * z_rows : (k + 1) * z_rows] = q_all[k, x_rows:]
    done_x = pltpu.make_async_copy(fx_ref, fx_out, ds.at[1])
    done_z = pltpu.make_async_copy(fz_ref, fz_out, ds.at[2])
    done_x.start()
    done_z.start()

    def close(m, carry):
        for d in range(1, nx):
            first(m, d).wait_send()
            second(m, d).wait_send()
        block(0, 3, m).wait()
        block(1, 3, m).wait_send()
        arrived(m, spot, 1 - core)

        @pl.when(middle)
        def _():
            raw(w_in.at[0, m], 2, m, last - spot).wait_send()

            @pl.when(m < late)
            def _():
                raw(w_own.at[m], 1, m, last - spot).wait_send()
                block(2, 3, m).wait_send()
                block(3, 3, m).wait_send()

            for slot in range(3):
                block(0, slot, m).wait()
                block(1, slot, m).wait_send()
                if slot:
                    block(2, slot, m).wait_send()
                    block(3, slot, m).wait_send()
                arrived(m, spots[slot], 1 - core)

        @pl.when(jnp.logical_not(middle))
        def _():
            raw(w_own.at[m], 0, m, near).wait_send()
            for d in range(1, ny // 2):
                for side in range(2):
                    at = lax.rem(spot + d, ny // 2)
                    here = jnp.logical_and(jnp.logical_and(at == near, side == core), m >= late)

                    @pl.when(jnp.logical_not(here))
                    def _(at=at, side=side):
                        arrived(m, at, side)

            @pl.when(m >= late)
            def _():
                block(0, 0, m, near).wait()
                block(1, 0, m, near).wait_send()

        return carry

    lax.fori_loop(0, steps, close, 0)
    for j in range(ahead):
        for d in range(1, nx):
            first(steps + j, d).wait_send()
            second(steps + j, d).wait_send()

    @pl.when(middle)
    def _():
        for j in range(ahead):
            early(j, 0).wait_send()
            early(j, 1).wait_send()

    for copy in (done_x, done_y, done_z):
        copy.wait()


def flow(field, gauss_east, gauss_up, east, north, up, nx, ny, a_in, lanes):
    rows, span, deep = field.shape
    a_rows = gauss_east.shape[0] // nx
    per_c = gauss_up.shape[0] // ny
    groups = a_rows // a_in
    tall = 8
    steps, share = span // tall, tall // nx
    ahead = 2
    most = steps + ahead
    width = up.shape[1]
    x_rows, z_rows = rows // ny, deep // ny
    lane = np.arange(lanes)
    used = lane < a_in * per_c
    sel = np.logical_and(lane[None] % per_c == np.arange(per_c)[:, None], used[None]).astype(np.float32)
    mask = (lane[None] // per_c == np.arange(a_in)[:, None]).astype(np.float32)
    total_k = sum(
        min((t * 128 + 127) // per_c, a_in - 1) + 1 - min(t * 128 // per_c, a_in - 1)
        for t in range(lanes // 128)
    ) * deep
    dma = lambda *shape: pltpu.SemaphoreType.DMA(shape)
    vm = pltpu.VMEM
    q_shape = (ny, x_rows + z_rows, width)
    batch = 16 if span % 16 == 0 else tall
    scratch = [
        vm((nx, a_rows, gauss_east.shape[1]), BF), vm(gauss_up.shape, BF), vm(sel.shape, BF),
        vm(mask.shape, F32), vm(east.shape, BF), vm(north.shape, BF), vm(up.shape, BF),
        vm((rows, width), F32), vm((deep, width), F32), vm((span, width), F32),
        vm((span // batch, rows, batch, deep), BF),
        vm((rows * batch, deep), F32),
        vm((span + ahead * tall, rows, deep), BF),
        vm((most, share, nx * rows, deep), BF),
        vm((most, nx - 1, a_rows, share * deep), BF),
        vm((most, nx, a_rows, share * deep), BF),
        vm((a_rows * tall, deep), F32),
        vm((most, groups * tall, a_in * deep), BF),
        vm((3, steps, groups * tall, a_in * deep), BF),
        vm((4, 4, steps, groups, tall, lanes), BF),
        vm((4, total_k, 128), BF),
        vm(q_shape, F32), vm(q_shape, F32), vm(q_shape, F32),
        vm((span, width), F32), vm((nx, span, width), F32),
        vm((nx, z_rows, width), F32), vm((z_rows, width), F32),
        dma(most, nx), dma(most, nx), dma(most), dma(most, nx), dma(most, nx),
        dma(2, ahead), dma(ahead),
        dma(3, steps), dma(3, steps), dma(4, 4, steps), dma(steps, ny // 2, 2), dma(4, steps),
        dma(span // batch), dma(7), dma(3),
        dma(ny), dma(ny), dma(nx), dma(nx), dma(nx), dma(nx), dma(ny), dma(ny),
    ]
    return pl.pallas_call(
        functools.partial(flow_kernel, nx, ny, per_c),
        out_shape=(
            pltpu.VMEM((groups, ny * span, lanes), BF),
            jax.ShapeDtypeStruct((rows, width), F32),
            jax.ShapeDtypeStruct((deep, width), F32),
            jax.ShapeDtypeStruct((span, width), F32),
        ),
        in_specs=[ANY] * 8,
        out_specs=(VMEM, ANY, ANY, ANY),
        scratch_shapes=scratch,
        compiler_params=pltpu.CompilerParams(collective_id=2, has_side_effects=True),
    )(
        field, gauss_east.reshape(nx, a_rows, -1), gauss_up,
        jnp.asarray(sel, BF), jnp.asarray(mask, F32), east, north, up,
    )


def mix_y_kernel(
    take, r_ref, g_ref, fx_ref, fy_ref, fz_ref, o_ref, fx_out, fy_out, fz_out,
    g_buf, o_buf, fx_buf, fy_buf, fz_buf, gs, os, fs, ts,
):
    groups = o_buf.shape[0]
    load = pltpu.make_async_copy(g_ref, g_buf, gs.at[0])
    load.start()
    trios = ((fx_ref, fx_buf, fx_out), (fy_ref, fy_buf, fy_out), (fz_ref, fz_buf, fz_out))
    ins = [pltpu.make_async_copy(src, mid, fs.at[k]) for k, (src, mid, _) in enumerate(trios)]
    stores = [pltpu.make_async_copy(mid, dst, ts.at[k]) for k, (_, mid, dst) in enumerate(trios)]
    for copy in ins:
        copy.start()
    load.wait()
    for c in range(0, groups, take):
        for k in range(c, c + take):
            o_buf[k] = lax.dot_general(
                r_ref[k], g_buf[...], (((0,), (1,)), ((), ())), preferred_element_type=F32
            )
        store = pltpu.make_async_copy(
            o_buf.at[pl.ds(c, take)], o_ref.at[pl.ds(c, take)], os.at[c // take]
        )
        store.start()
        stores.append(store)
        if c == 0:
            for k in range(3):
                ins[k].wait()
                stores[k].start()
    for copy in stores:
        copy.wait()


def mix_y(r, g, fx, fy, fz):
    groups, deep, lanes = r.shape
    out = g.shape[0]
    take = 1 if groups % 1 == 0 else 1
    dma = lambda *shape: pltpu.SemaphoreType.DMA(shape)
    vm = pltpu.VMEM
    like = lambda x: jax.ShapeDtypeStruct(x.shape, x.dtype)
    return pl.pallas_call(
        functools.partial(mix_y_kernel, take),
        out_shape=(jax.ShapeDtypeStruct((groups, lanes, out), F32), like(fx), like(fy), like(fz)),
        in_specs=[VMEM, ANY, ANY, ANY, ANY],
        out_specs=(ANY, ANY, ANY, ANY),
        scratch_shapes=[
            vm(g.shape, BF), vm((groups, lanes, out), F32), vm(fx.shape, F32), vm(fy.shape, F32),
            vm(fz.shape, F32), dma(1), dma(groups // take), dma(3), dma(3),
        ],
    )(r, g, fx, fy, fz)


def per_device(
    nx, ny,
    thermal_field,
    probe_range_east,
    probe_range_north,
    probe_range_upward,
    gauss_kernel_east,
    gauss_kernel_north,
    gauss_kernel_upward,
):
    rows, span, deep = thermal_field.shape
    a_rows = gauss_kernel_east.shape[0] // nx
    per_c = gauss_kernel_upward.shape[0] // ny
    a_in = 8 if a_rows % 8 == 0 and 8 * per_c % 128 == 0 else a_rows
    groups = a_rows // a_in
    used = a_in * per_c
    lanes = -(-used // 128) * 128

    if ny == 8 and 8 % nx == 0 and span % 8 == 0 and span // 8 > 5 and a_in % 8 == 0 and per_c % 16 == 0:
        r, factor_x, factor_z, factor_y = flow(
            thermal_field, gauss_kernel_east, gauss_kernel_upward,
            probe_range_east, probe_range_north, probe_range_upward, nx, ny, a_in, lanes,
        )
        r = pltpu.with_memory_space_constraint(r, pltpu.VMEM)
    else:
        w, q, part_y = mix_x(
            thermal_field.reshape(rows, span * deep),
            gauss_kernel_east.reshape(nx, a_rows, -1),
            nx,
            a_rows,
            thermal_field,
            probe_range_east,
            probe_range_north,
            probe_range_upward,
            ny,
        )
        w = w.reshape(groups, a_in, span, deep).transpose(0, 2, 1, 3).reshape(groups * span, a_in * deep)

        gt = gauss_kernel_upward.reshape(ny, per_c, deep).transpose(0, 2, 1)
        gt = jnp.pad(jnp.tile(gt, (1, 1, a_in)), ((0, 0), (0, 0), (0, lanes - used)))
        mask = (
            lax.broadcasted_iota(jnp.int32, (a_in, lanes), 1) // per_c
            == lax.broadcasted_iota(jnp.int32, (a_in, lanes), 0)
        ).astype(BF)
        r, factor_x, factor_z, factor_y = exchange(w, gt, mask, q, part_y, nx, ny, groups, span, per_c)

    core, factor_x, factor_y, factor_z = mix_y(r, gauss_kernel_north, factor_x, factor_y, factor_z)
    core = core[:, :used].reshape(a_rows, per_c, -1).transpose(0, 2, 1)
    return (factor_x, factor_y, factor_z, core)


def solution(mesh):
    in_specs = (P("gx", "gy", None), P("gx", None), P("gy", None), P(), P(), P(), P())
    out_specs = (P("gx", None), P("gy", None), P(), P("gx", None, "gy"))
    body = functools.partial(per_device, mesh.shape["gx"], mesh.shape["gy"])
    return jax.shard_map(
        body, mesh=mesh, in_specs=in_specs, out_specs=out_specs, check_vma=False
    )
```
